32 devices in a mesh: gy: 8 (over y, x, core), gz: 4 (over z).
Axes of the slice: x: 2, y: 2, z: 4, core: 2. Of those that a mesh axis runs over, the one named last changes fastest.
Arguments:
- magnetic: float32 [3, 192, 32, 256], P(None, 'gy', 'gz'), may hold values from -6 to 6
- velocity: float32 [3, 192, 32, 256], P(None, 'gy', 'gz'), may hold values from -6 to 6
- diffusivity: float32 [192, 32, 256], P('gy', 'gz'), may hold values from 0.5 to 2
- material: int32 [192, 32, 256], P('gy', 'gz'), may hold values 0 or 1
- plane_rate: float32 [32], P('gz'), may hold values from 0.5 to 2000
- cotangent: float32 [3, 192, 32, 256], P(None, 'gy', 'gz'), may hold values from -6 to 6
Outputs:
- new_field: float32 [3, 192, 32, 256], P(None, 'gy', 'gz')
- adjoint_field: float32 [3, 192, 32, 256], P(None, 'gy', 'gz')
The draws below stay inside these ranges and needn't reach their ends.
Inputs may be any that keep to these rules, and one draw needn't show every extreme that they name: `material`: 1 marks impeller iron.
All inputs are finite; a program needn't handle non-finite values. No bound on the sum of `material` on one device may be relied on, other than what follows from the above.
Results may differ from the reference program's by a relative error of at most 0.000098.
Values sent between devices are 32-bit elements; how exact they have to be, the bound alone decides.
A program may use at most 64 MiB of HBM per device.

```python
import math
import jax
import jax.numpy as jnp
from jax import lax

CY = 24
NX = 256
NY = 192
NZ = 32


def place_ends(array, own_key, least, high):
    index_at = [jax.random.randint(jax.random.fold_in(own_key, axis), (), 0, length) for axis, length in enumerate(array.shape)]
    widest = array.shape.index(max(array.shape))
    beside = index_at[:widest] + [(index_at[widest] + 1) % array.shape[widest]] + index_at[widest + 1:]
    return array.at[tuple(index_at)].set(least).at[tuple(beside)].set(high)


def level_of(key, extent, cuts, low, top_value):
    level = 1.0
    for dim, blocks in cuts:
        heights = jax.random.uniform(jax.random.fold_in(jax.random.fold_in(key, 6), dim), (blocks,), jnp.float32, low / len(cuts), top_value / len(cuts))
        level = level * jnp.repeat(jnp.exp(heights), extent[dim] // blocks).reshape((-1,) + (1,) * (len(extent) - 1 - dim))
    return level


def noise(key, dims, width, most, cuts=(), kind=jnp.bfloat16):
    loudness = level_of(key, dims, cuts, -0.22, 0.18) if cuts else 1.0
    values = jax.random.normal(key, dims, jnp.float32) * width * loudness
    return jnp.minimum(jnp.maximum(values, -most), most).astype(kind)


def setup_inputs(seed: int = 0) -> dict:
    arg_keys = jax.random.split(jax.random.key(seed), 7)
    magnetic = noise(arg_keys[0], (3, NY, NZ, NX), 1.0, 6.0, ((1, 8), (2, 4)), jnp.float32)
    velocity = noise(arg_keys[1], (3, NY, NZ, NX), 1.0, 6.0, ((1, 8), (2, 4)), jnp.float32)
    diffusivity = jnp.clip(jnp.exp(math.log(2.0) - 1.3862944 * jax.random.uniform(arg_keys[2], (NY, NZ, NX), jnp.float32) ** level_of(arg_keys[2], (NY, NZ, NX), ((0, 8), (1, 4)), -0.2, 0.2)), 0.5, 2.0)
    material = place_ends((jax.random.randint(arg_keys[3], (NY, NZ, NX), 0, 4) < 1).astype(jnp.int32), jax.random.fold_in(arg_keys[3], 1), 0, 1)
    plane_rate = jnp.clip(jnp.exp(math.log(2000.0) - 8.2940496 * jax.random.uniform(arg_keys[4], (NZ,), jnp.float32) ** level_of(arg_keys[4], (NZ,), ((0, 4),), -0.2, 0.2)), 0.5, 2000.0)
    cotangent = noise(arg_keys[5], (3, NY, NZ, NX), 1.0, 6.0, ((1, 8), (2, 4)), jnp.float32)
    return dict(magnetic=magnetic, velocity=velocity, diffusivity=diffusivity, material=material, plane_rate=plane_rate, cotangent=cotangent)


step_size = 0.1
iron_factor = 0.2

def slope_y(vector):
    return 0.5 * (vector[:, 2:, 1:-1] - vector[:, :-2, 1:-1])

def slope_z(vector):
    return 0.5 * (vector[:, 1:-1, 2:] - vector[:, 1:-1, :-2])

def slope_x(vector):
    inner = vector[:, 1:-1, 1:-1]
    padded = jnp.pad(inner, ((0, 0), (0, 0), (0, 0), (1, 1)))
    return 0.5 * (padded[..., 2:] - padded[..., :-2])

def curl_of(vector):
    along_y = slope_y(vector)
    along_z = slope_z(vector)
    along_x = slope_x(vector)
    return jnp.stack([along_y[2] - along_z[1], along_z[0] - along_x[2], along_x[1] - along_y[0]])

def induction(padded, coefficients):
    inner = padded[:, 1:-1, 1:-1]
    speed = coefficients[:3]
    spread = coefficients[3]
    crossed = jnp.stack([speed[1] * inner[2] - speed[2] * inner[1], speed[2] * inner[0] - speed[0] * inner[2], speed[0] * inner[1] - speed[1] * inner[0]])
    return curl_of(crossed - spread[None] * curl_of(padded))

def line_solve_ref(line_values, plane_rate):
    stacked = jnp.transpose(line_values, (2, 1, 0, 3)).reshape(NZ, NY, 3 * NX)
    rate_grid = plane_rate[:, None] * jnp.ones((1, NY), jnp.float32)
    lower_band = (-rate_grid).at[:, 0].set(0.0)
    upper_band = (-rate_grid).at[:, -1].set(0.0)
    middle = 1.0 + 2.0 * rate_grid
    solved = lax.linalg.tridiagonal_solve(lower_band, middle, upper_band, stacked)
    return jnp.transpose(solved.reshape(NZ, NY, 3, NX), (2, 1, 0, 3))

def reference(magnetic, velocity, diffusivity, material, plane_rate, cotangent):
    spread = diffusivity * (1.0 - (1.0 - iron_factor) * material.astype(jnp.float32))
    coefficients = jnp.concatenate([velocity, spread[None]], axis=0)
    field_pad = jnp.pad(magnetic, ((0, 0), (4, 4), (4, 4), (0, 0)))
    coef_pad = jnp.pad(coefficients, ((0, 0), (3, 3), (3, 3), (0, 0)))
    starts = jnp.arange(NY // CY, dtype=jnp.int32) * CY

    def forward_block(row_start):
        slab_part = lax.dynamic_slice_in_dim(field_pad, row_start + 2, CY + 4, 1)[:, :, 2:-2]
        near_coef = lax.dynamic_slice_in_dim(coef_pad, row_start + 2, CY + 2, 1)[:, :, 2:-2]
        return induction(slab_part, near_coef)
    change = lax.map(forward_block, starts)
    change = jnp.moveaxis(change, 0, 1).reshape(3, NY, NZ, NX)
    advanced = magnetic + step_size * change
    new_field = line_solve_ref(advanced, plane_rate)
    relaxed = line_solve_ref(cotangent, plane_rate)
    weight_pad = jnp.pad(relaxed, ((0, 0), (2, 2), (2, 2), (0, 0)))

    def adjoint_block(row_start):
        near_coef = lax.dynamic_slice_in_dim(coef_pad, row_start, CY + 6, 1)
        seen_weight = lax.dynamic_slice_in_dim(weight_pad, row_start, CY + 4, 1)
        zero_field = jnp.zeros((3, CY + 8, NZ + 8, NX), jnp.float32)
        outcome, pullback = jax.vjp(lambda probe: induction(probe, near_coef), zero_field)
        return pullback(seen_weight)[0][:, 4:-4, 4:-4]
    pulled = lax.map(adjoint_block, starts)
    pulled = jnp.moveaxis(pulled, 0, 1).reshape(3, NY, NZ, NX)
    adjoint_field = relaxed + step_size * pulled
    return (new_field, adjoint_field)
```

```python
import functools
import jax
import jax.numpy as jnp
from jax import lax
from jax.experimental import pallas as pl
from jax.experimental.pallas import tpu as pltpu
from jax.sharding import PartitionSpec as P

step_size = 0.1
iron_factor = 0.2
MESH = pl.DeviceIdType.MESH
LANES = 128
SIDES = ((0, -1), (1, 1))
N_MOVES = 20
G_COMPS = (0, 1, 3)
SPREAD = 2


def kernel(
    groups, layers, n, mag, vel, dif, mat, rate, cot, new, adj,
    bE, gE, wE, hE, v, iron, rate_row, zb, zg, zw, zh, yb, yc, yg, yk, ends, sums,
    m_tab, inv_tab, al_tab, s_tab, den_tab, w_tab, mix, coef,
    load_sem, send_sem, recv_sem, gs_sem, gr_sem,
):
    me = lax.axis_index("gy")
    lay = lax.axis_index("gz")
    nx = bE.shape[-1]
    nz = bE.shape[-2]
    half = 0.5 * step_size

    rate_load = pltpu.make_async_copy(rate, rate_row, load_sem.at[5])
    rate_load.start()
    loads = [
        pltpu.make_async_copy(dif, gE.at[SPREAD, pl.ds(1, n)], load_sem.at[3]),
        pltpu.make_async_copy(mat, iron, load_sem.at[4]),
        pltpu.make_async_copy(mag, bE.at[:, pl.ds(1, n)], load_sem.at[0]),
        pltpu.make_async_copy(vel, v, load_sem.at[2]),
        pltpu.make_async_copy(cot, wE.at[:, pl.ds(1, n)], load_sem.at[1]),
    ]
    for load in loads:
        load.start()

    has_left, has_right = me > 0, me < groups - 1
    has_low, has_high = lay > 0, lay < layers - 1

    def there(dy, dz):
        found = None
        for step, low, high in ((dy, has_left, has_right), (dz, has_low, has_high)):
            if step:
                seen = low if step < 0 else high
                found = seen if found is None else jnp.logical_and(found, seen)
        return found

    def place(dy, dz):
        return {
            "gy": jnp.clip(me + dy, 0, groups - 1) if dy else me,
            "gz": jnp.clip(lay + dz, 0, layers - 1) if dz else lay,
        }

    around = [(dy, dz) for dy in (-1, 0, 1) for dz in (-1, 0, 1) if dz]
    barrier = pltpu.get_barrier_semaphore()
    for k in range(1, groups):
        pl.semaphore_signal(
            barrier, inc=1, device_id={"gy": lax.rem(me + k, groups), "gz": lay}, device_id_type=MESH
        )
    count = jnp.int32(groups - 1)
    for dy, dz in around:
        count = count + there(dy, dz).astype(jnp.int32)

        @pl.when(there(dy, dz))
        def _():
            pl.semaphore_signal(barrier, inc=1, device_id=place(dy, dz), device_id_type=MESH)

    def move(slot, src, dst, dy, dz):
        copy = pltpu.make_async_remote_copy(
            src_ref=src, dst_ref=dst, send_sem=send_sem.at[slot], recv_sem=recv_sem.at[slot],
            device_id=place(dy, dz), device_id_type=MESH)
        return copy, there(dy, dz), there(-dy, -dz)

    def start(moves):
        for copy, ahead, _ in moves:
            @pl.when(ahead)
            def _():
                copy.start()

    def arrive(moves):
        for copy, _, behind in moves:
            @pl.when(behind)
            def _():
                copy.wait_recv()

    def leave(moves):
        for copy, ahead, _ in moves:
            @pl.when(ahead)
            def _():
                copy.wait_send()

    Y_WAYS = ((-1, 0, 1), (1, n - 1, 0))
    Z_WAYS = ((-1, 0, nz - 1), (1, nz - 1, 0))

    def y_moves(slot, src, dst, first):
        return [
            move(slot + i, src(first + row), dst(side), dy, 0)
            for i, (dy, row, side) in enumerate(Y_WAYS)
        ]

    def z_moves(slot, src, dst):
        return [
            move(slot + i, src(pl.ds(mine, 1)), dst(pl.ds(theirs, 1)), 0, dz)
            for i, (dz, mine, theirs) in enumerate(Z_WAYS)
        ]

    yb_moves = y_moves(0, lambda row: mag.at[:, row], lambda side: yb.at[side], 0)
    yc_moves = y_moves(2, lambda row: cot.at[:, row], lambda side: yc.at[side], 0)
    yg_moves = y_moves(4, lambda row: gE.at[:, row], lambda side: yg.at[side], 1)
    yk_moves = [
        move(
            6 + 2 * i + j, mag.at[pl.ds(1, 2), row, pl.ds(mine, 1)], yk.at[side, :, pl.ds(theirs, 1)], dy, dz
        )
        for i, (dy, row, side) in enumerate(Y_WAYS)
        for j, (dz, mine, theirs) in enumerate(Z_WAYS)
    ]
    both = pl.ds(0, 2)
    zb_moves = z_moves(10, lambda z: mag.at[both, :, z], lambda z: zb.at[:, :, z])
    zg_moves = z_moves(12, lambda z: gE.at[pl.ds(0, 3), pl.ds(1, n), z], lambda z: zg.at[:, :, z])
    zw_moves = z_moves(14, lambda z: wE.at[both, :, z], lambda z: zw.at[:, :, z])
    zh_moves = z_moves(16, lambda z: hE.at[both, pl.ds(1, n), z], lambda z: zh.at[:, :, z])

    pl.semaphore_wait(barrier, count)
    start(zb_moves)
    start(yb_moves)
    start(yk_moves)
    start(yc_moves)

    zero = jnp.zeros((nz, nx), jnp.float32)
    for part in (0, 2):
        bE[part, 0] = zero
        bE[part, n + 1] = zero

    def wide(tile):
        return jnp.concatenate([tile] * (nx // LANES), axis=1)

    lane = lax.broadcasted_iota(jnp.int32, (nz, LANES), 1)
    sub = wide(lax.broadcasted_iota(jnp.int32, (nz, LANES), 0))
    flag = jnp.where(
        sub == nz - 1, has_high.astype(jnp.int32), jnp.where(sub == 0, has_low.astype(jnp.int32), 0)
    )
    active = flag > 0
    sign = jnp.where(sub == 0, -1.0, 1.0)

    def rim(halo):
        return jnp.where(active, sign * halo, 0.0)

    square = (
        lax.broadcasted_iota(jnp.int32, (nz, nz), 0) == lax.broadcasted_iota(jnp.int32, (nz, nz), 1)
    )
    rate_load.wait()
    r = jnp.sum(jnp.where(square, jnp.broadcast_to(rate_row[...], (nz, nz)), 0.0), axis=1, keepdims=True)
    r = jnp.broadcast_to(r, (nz, LANES))
    one = jnp.ones((nz, LANES), jnp.float32)

    r_inv = 1.0 / r
    whole, grown = one, one
    sizes = [one]
    for k in range(n):
        grown = grown + r_inv * whole
        whole = whole + grown
        sizes.append(whole)
    full_inv = 1.0 / whole
    for k in range(n):
        m = sizes[k] / sizes[k + 1]
        m_tab[k] = m
        inv_tab[k] = m * r_inv
        al_tab[n - 1 - k] = sizes[k] * full_inv
    aa, cc = sizes[n - 1] * full_inv, full_inv

    def reach(k, s):
        s_tab[k] = s
        den = cc / (1.0 - s * aa)
        den_tab[k] = den
        return aa + cc * s * den

    lax.fori_loop(0, groups, reach, jnp.zeros((nz, LANES), jnp.float32), unroll=groups <= 8)
    s_low, s_high = s_tab[me], s_tab[groups - 1 - me]
    from_low, from_high = den_tab[me] * s_low, den_tab[groups - 1 - me] * s_high
    for k in range(n):
        near, far = al_tab[k] * r_inv, al_tab[n - 1 - k] * r_inv
        w_tab[0, k] = far + from_low * near
        w_tab[1, k] = near + from_high * far

    def gather(slot):
        copies = []
        for k in range(1, groups):
            partner = lax.rem(me + k, groups)
            copies.append(pltpu.make_async_remote_copy(
                src_ref=sums.at[slot, (partner < me).astype(jnp.int32)], dst_ref=ends.at[slot, k - 1],
                send_sem=gs_sem.at[slot, k - 1], recv_sem=gr_sem.at[slot, k - 1],
                device_id={"gy": partner, "gz": lay}, device_id_type=MESH,
            ))
        return copies

    nothing = (zero,) * 6

    def collect(totals, k, rows):
        toward = (wide(w_tab[0, k]), wide(w_tab[1, k]))
        return tuple(totals[3 * way + c] + toward[way] * rows[c] for way in range(2) for c in range(3))

    def put_sums(slot, totals):
        for way in range(2):
            for c in range(3):
                sums[slot, way, c] = totals[3 * way + c]

    def slope_x(f):
        tiles = [f[:, at:at + LANES] for at in range(0, nx, LANES)]
        ahead = [pltpu.roll(tile, LANES - 1, 1) for tile in tiles] + [jnp.zeros_like(tiles[0])]
        behind = [jnp.zeros_like(tiles[0])] + [pltpu.roll(tile, 1, 1) for tile in tiles]
        return jnp.concatenate(
            [
                jnp.where(lane == LANES - 1, ahead[t + 1], ahead[t])
                - jnp.where(lane == 0, behind[t], behind[t + 1])
                for t in range(len(tiles))
            ],
            axis=1,
        )

    def slope_z(f):
        ahead = jnp.where(sub == nz - 1, 0.0, pltpu.roll(f, nz - 1, 0))
        behind = jnp.where(sub == 0, 0.0, pltpu.roll(f, 1, 0))
        return ahead - behind

    def curl(field, y, extra=None, comps=(0, 1, 2)):
        f = [field[c, y + 1] for c in comps]
        dy_x = field[comps[0], y + 2] - field[comps[0], y]
        dy_z = field[comps[2], y + 2] - field[comps[2], y]
        dz_x, dz_y = slope_z(f[0]), slope_z(f[1])
        if extra is not None:
            dz_x, dz_y = dz_x + extra[0], dz_y + extra[1]
        return (dy_z - dz_y, dz_x - slope_x(f[2]), slope_x(f[1]) - dy_x), f

    def each_row(body):
        for y in range(n):
            body(y)

    for load in loads[:4]:
        load.wait()

    def argument(y):
        turn, b = curl(bE, y)
        s = [v[c, y] for c in range(3)]
        sp = gE[SPREAD, y + 1] * (0.5 - 0.5 * (1.0 - iron_factor) * iron[y].astype(jnp.float32))
        gE[0, y + 1] = s[1] * b[2] - s[2] * b[1] - sp * turn[0]
        gE[1, y + 1] = s[2] * b[0] - s[0] * b[2] - sp * turn[1]
        gE[SPREAD, y + 1] = sp
        gE[3, y + 1] = s[0] * b[1] - s[1] * b[0] - sp * turn[2]

    each_row(argument)
    start(zg_moves)
    start(yg_moves)

    loads[4].wait()
    totals = nothing
    for k in range(n):
        totals = collect(totals, k, [wE[c, k + 1] for c in range(3)])
    put_sums(0, totals)
    for copy in gather(0):
        copy.start()

    def local_solve(field, offset):
        def down(k, held):
            m = wide(m_tab[jnp.maximum(k - 1, 0)])
            rows = tuple(field[c, offset + k] + m * held[c] for c in range(3))
            for c in range(3):
                field[c, offset + k] = rows[c]
            return rows

        lax.fori_loop(0, n, down, (zero, zero, zero), unroll=True)

        def up(step, held):
            k = n - 1 - step
            m, inv = wide(m_tab[k]), wide(inv_tab[k])
            rows = tuple(field[c, offset + k] * inv + m * held[c] for c in range(3))
            for c in range(3):
                field[c, offset + k] = rows[c]
            return rows

        lax.fori_loop(0, n, up, (zero, zero, zero), unroll=True)

    left_gap, right_gap = 1.0 - s_low * aa, 1.0 - s_high * aa
    det = 1.0 / (left_gap * right_gap - s_low * s_high * cc * cc)
    ll, lr = right_gap * det, s_low * cc * det
    rr, rl = left_gap * det, s_high * cc * det
    mix[0] = ll * s_low
    mix[1] = lr * s_high
    mix[2] = rl * s_low
    mix[3] = rr * s_high
    low = one
    for k in range(1, groups):
        @pl.when(k <= me)
        def _(low=low):
            coef[0, k - 1] = ll * low
            coef[1, k - 1] = rl * low

        low = low * den_tab[jnp.maximum(me - k, 0)]
    high = one
    for k in range(1, groups):
        @pl.when(k <= groups - 1 - me)
        def _(high=high):
            coef[0, groups - k - 1] = lr * high
            coef[1, groups - k - 1] = rr * high

        high = high * den_tab[jnp.maximum(groups - 1 - me - k, 0)]

    local_solve(wE, 1)

    def gather_wait(slot):
        for copy in gather(slot):
            copy.wait_recv()

    def interface(slot, field, offset):
        first = [field[c, offset] for c in range(3)]
        last = [field[c, offset + n - 1] for c in range(3)]
        lefts, rights = [], []
        for c in range(3):
            left = wide(mix[0]) * first[c] + wide(mix[1]) * last[c]
            right = wide(mix[2]) * first[c] + wide(mix[3]) * last[c]
            for k in range(groups - 1):
                end = ends[slot, k, c]
                left = left + wide(coef[0, k]) * end
                right = right + wide(coef[1, k]) * end
            lefts.append(left)
            rights.append(right)
        return lefts, rights

    arrive(zb_moves + yb_moves + yk_moves + yg_moves + zg_moves)
    leave(yg_moves + zg_moves)

    for side, way in SIDES:
        have = (has_left, has_right)[side]
        edge, halo, y = (1, 0, 0) if side == 0 else (n, n + 1, n - 1)
        beyond, sp = way * yg[side, SPREAD], way * gE[SPREAD, edge]
        g_x = yg[side, 0] + beyond * (bE[2, edge] + way * rim(yk[side, 0]))
        g_z = yg[side, 3] - beyond * bE[0, edge]
        gE[0, halo] = jnp.where(have, g_x, 0.0)
        gE[3, halo] = jnp.where(have, g_z, 0.0)
        gE[0, edge] = gE[0, edge] - jnp.where(have, sp * yb[side, 2], 0.0)
        gE[3, edge] = gE[3, edge] + jnp.where(have, sp * yb[side, 0], 0.0)
        zg[0, y] = zg[0, y] - jnp.where(have, way * zg[SPREAD, y] * yk[side, 1], 0.0)

    def mend_argument(y):
        sp = gE[SPREAD, y + 1]
        gE[0, y + 1] = gE[0, y + 1] + sp * rim(zb[1, y])
        gE[1, y + 1] = gE[1, y + 1] - sp * rim(zb[0, y])

    each_row(mend_argument)

    totals = nothing
    for y in range(n):
        b = [bE[c, y + 1] for c in range(3)]
        sp = zg[SPREAD, y]
        extra = (
            jnp.where(active, sign * zg[0, y] - sp * b[1], 0.0),
            jnp.where(active, sign * zg[1, y] + sp * b[0], 0.0),
        )
        turn, _ = curl(gE, y, extra, G_COMPS)
        rows = [b[c] + half * turn[c] for c in range(3)]
        for c in range(3):
            new[c, y] = rows[c]
        totals = collect(totals, y, rows)
    put_sums(1, totals)
    for copy in gather(1):
        copy.start()

    gather_wait(0)
    lefts, rights = interface(0, wE, 1)
    for c in range(3):
        wE[c, 0] = lefts[c]
        wE[c, n + 1] = rights[c]

    def relax(y):
        near, far = wide(al_tab[y]), wide(al_tab[n - 1 - y])
        for c in range(3):
            wE[c, y + 1] = wE[c, y + 1] + near * wE[c, 0] + far * wE[c, n + 1]

    each_row(relax)
    start(zw_moves)

    def pull(y):
        turn, w = curl(wE, y)
        s = [v[c, y] for c in range(3)]
        sp = gE[SPREAD, y + 1]
        adj[0, y] = w[0] + half * (turn[1] * s[2] - turn[2] * s[1])
        adj[1, y] = w[1] + half * (turn[2] * s[0] - turn[0] * s[2])
        adj[2, y] = w[2] + half * (turn[0] * s[1] - turn[1] * s[0])
        for c in range(3):
            hE[c, y + 1] = sp * turn[c]

    each_row(pull)
    start(zh_moves)

    arrive(yc_moves)
    wide_inv = wide(r_inv)
    for side, way in SIDES:
        have = (has_left, has_right)[side]
        edge, halo = (1, 0) if side == 0 else (n, n + 1)
        sp = yg[side, SPREAD]
        slope = {}
        for c in (0, 2):
            near, rim_row = wE[c, edge], wE[c, halo]
            outer = rim_row + (rim_row - near) + wide_inv * (rim_row - yc[side, c])
            slope[c] = way * (outer - near)
        cross = wE[1, halo]
        hE[0, halo] = jnp.where(have, sp * (slope[2] - slope_z(cross)), 0.0)
        hE[2, halo] = jnp.where(have, sp * (slope_x(cross) - slope[0]), 0.0)

    local_solve(new, 0)
    gather_wait(1)
    lefts, rights = interface(1, new, 0)

    def finish(y):
        near, far = wide(al_tab[y]), wide(al_tab[n - 1 - y])
        for c in range(3):
            new[c, y] = new[c, y] + near * lefts[c] + far * rights[c]

    each_row(finish)

    arrive(zw_moves + zh_moves)
    leave(zh_moves)

    for side, way in SIDES:
        have = (has_left, has_right)[side]
        halo = 0 if side == 0 else n + 1
        hE[0, halo] = hE[0, halo] - jnp.where(have, yg[side, SPREAD] * rim(zw[1, halo]), 0.0)

    def mend_pull(y):
        c_x, c_y = rim(zw[0, y + 1]), rim(zw[1, y + 1])
        sp = gE[SPREAD, y + 1]
        s = [v[c, y] for c in range(3)]
        hE[0, y + 1] = hE[0, y + 1] - sp * c_y
        hE[1, y + 1] = hE[1, y + 1] + sp * c_x
        h_x, h_y = half * c_x, half * c_y
        adj[0, y] = adj[0, y] + h_x * s[2]
        adj[1, y] = adj[1, y] + h_y * s[2]
        adj[2, y] = adj[2, y] - (h_y * s[1] + h_x * s[0])

    each_row(mend_pull)

    def finish_adjoint(y):
        sp = zg[SPREAD, y]
        extra = (
            jnp.where(active, sign * zh[0, y] + sp * wE[1, y + 1], 0.0),
            jnp.where(active, sign * zh[1, y] - sp * wE[0, y + 1], 0.0),
        )
        turn, _ = curl(hE, y, extra)
        for c in range(3):
            adj[c, y] = adj[c, y] - half * turn[c]

    each_row(finish_adjoint)

    leave(yb_moves + yc_moves + yk_moves + zb_moves + zw_moves)
    for slot in range(2):
        for copy in gather(slot):
            copy.wait_send()


def hand_over(new, adj, new_out, adj_out, sem):
    copies = [
        pltpu.make_async_copy(new, new_out, sem.at[0]),
        pltpu.make_async_copy(adj, adj_out, sem.at[1]),
    ]
    for copy in copies:
        copy.start()
    for copy in copies:
        copy.wait()


def local(groups, layers, magnetic, velocity, diffusivity, material, plane_rate, cotangent):
    _, n, nz, nx = magnetic.shape
    block = (3, n, nz, nx)
    rimmed = (3, n + 2, nz, nx)
    f32 = jnp.float32
    anywhere = pl.BlockSpec(memory_space=pl.ANY)
    inside = pl.BlockSpec(memory_space=pltpu.VMEM)
    args = [
        pltpu.with_memory_space_constraint(array, pltpu.HBM)
        for array in (magnetic, velocity, diffusivity, material, plane_rate.reshape(1, nz), cotangent)
    ]
    new, adj = pl.pallas_call(
        functools.partial(kernel, groups, layers, n),
        out_shape=[jax.ShapeDtypeStruct(block, f32)] * 2,
        in_specs=[anywhere] * 6,
        out_specs=[inside] * 2,
        scratch_shapes=[
            pltpu.VMEM(rimmed, f32),
            pltpu.VMEM((4, n + 2, nz, nx), f32),
            pltpu.VMEM(rimmed, f32),
            pltpu.VMEM(rimmed, f32),
            pltpu.VMEM(block, f32),
            pltpu.VMEM((n, nz, nx), jnp.int32),
            pltpu.VMEM((1, nz), f32),
            pltpu.VMEM((2, n, nz, nx), f32),
            pltpu.VMEM((3, n, nz, nx), f32),
            pltpu.VMEM((2, n + 2, nz, nx), f32),
            pltpu.VMEM((2, n, nz, nx), f32),
            pltpu.VMEM((2, 3, nz, nx), f32),
            pltpu.VMEM((2, 3, nz, nx), f32),
            pltpu.VMEM((2, 4, nz, nx), f32),
            pltpu.VMEM((2, 2, nz, nx), f32),
            pltpu.VMEM((2, groups - 1, 3, nz, nx), f32),
            pltpu.VMEM((2, 2, 3, nz, nx), f32),
            pltpu.VMEM((n, nz, LANES), f32),
            pltpu.VMEM((n, nz, LANES), f32),
            pltpu.VMEM((n, nz, LANES), f32),
            pltpu.VMEM((groups, nz, LANES), f32),
            pltpu.VMEM((groups, nz, LANES), f32),
            pltpu.VMEM((2, n, nz, LANES), f32),
            pltpu.VMEM((4, nz, LANES), f32),
            pltpu.VMEM((2, groups - 1, nz, LANES), f32),
            pltpu.SemaphoreType.DMA((6,)),
            pltpu.SemaphoreType.DMA((N_MOVES,)),
            pltpu.SemaphoreType.DMA((N_MOVES,)),
            pltpu.SemaphoreType.DMA((2, groups - 1)),
            pltpu.SemaphoreType.DMA((2, groups - 1)),
        ],
        compiler_params=pltpu.CompilerParams(
            collective_id=0, has_side_effects=True, vmem_limit_bytes=24 * 2**20
        ),
    )(*args)
    return tuple(pl.pallas_call(
        hand_over,
        out_shape=[jax.ShapeDtypeStruct(block, f32)] * 2,
        in_specs=[anywhere] * 2,
        out_specs=[anywhere] * 2,
        scratch_shapes=[pltpu.SemaphoreType.DMA((2,))],
        compiler_params=pltpu.CompilerParams(vmem_limit_bytes=2**20),
    )(new, adj))


def solution(mesh):
    in_specs = (
        P(None, "gy", "gz", None),
        P(None, "gy", "gz", None),
        P("gy", "gz", None),
        P("gy", "gz", None),
        P("gz"),
        P(None, "gy", "gz", None),
    )
    out_specs = (P(None, "gy", "gz", None), P(None, "gy", "gz", None))
    body = functools.partial(local, mesh.shape["gy"], mesh.shape["gz"])
    return jax.shard_map(body, mesh=mesh, in_specs=in_specs, out_specs=out_specs, check_vma=False)
```

```python
import functools
import jax
import jax.numpy as jnp
from jax import lax
from jax.experimental import pallas as pl
from jax.experimental.pallas import tpu as pltpu
from jax.sharding import PartitionSpec as P

step_size = 0.1
iron_factor = 0.2
MESH = pl.DeviceIdType.MESH
LANES = 128
SIDES = ((0, -1), (1, 1))
N_MOVES = 20
G_COMPS = (0, 1, 3)
SPREAD = 2


def kernel(
    groups, layers, n, mag, vel, dif, mat, rate, cot, new, adj,
    bE, gE, wE, hE, v, iron, rate_row, zb, zg, zw, zh, yb, yc, yg, yk, ends, sums,
    m_tab, inv_tab, al_tab, s_tab, den_tab, w_tab, mix, coef,
    load_sem, send_sem, recv_sem, gs_sem, gr_sem,
):
    me = lax.axis_index("gy")
    lay = lax.axis_index("gz")
    nx = bE.shape[-1]
    nz = bE.shape[-2]
    half = 0.5 * step_size

    rate_load = pltpu.make_async_copy(rate, rate_row, load_sem.at[5])
    rate_load.start()
    loads = [
        pltpu.make_async_copy(cot, wE.at[:, pl.ds(1, n)], load_sem.at[1]),
        pltpu.make_async_copy(mag, bE.at[:, pl.ds(1, n)], load_sem.at[0]),
        pltpu.make_async_copy(dif, gE.at[SPREAD, pl.ds(1, n)], load_sem.at[3]),
        pltpu.make_async_copy(mat, iron, load_sem.at[4]),
        pltpu.make_async_copy(vel, v, load_sem.at[2]),
    ]
    for load in loads:
        load.start()

    has_left, has_right = me > 0, me < groups - 1
    has_low, has_high = lay > 0, lay < layers - 1

    def there(dy, dz):
        found = None
        for step, low, high in ((dy, has_left, has_right), (dz, has_low, has_high)):
            if step:
                seen = low if step < 0 else high
                found = seen if found is None else jnp.logical_and(found, seen)
        return found

    def place(dy, dz):
        return {
            "gy": jnp.clip(me + dy, 0, groups - 1) if dy else me,
            "gz": jnp.clip(lay + dz, 0, layers - 1) if dz else lay,
        }

    around = [(dy, dz) for dy in (-1, 0, 1) for dz in (-1, 0, 1) if dz]
    barrier = pltpu.get_barrier_semaphore()
    for k in range(1, groups):
        pl.semaphore_signal(
            barrier, inc=1, device_id={"gy": lax.rem(me + k, groups), "gz": lay}, device_id_type=MESH
        )
    count = jnp.int32(groups - 1)
    for dy, dz in around:
        count = count + there(dy, dz).astype(jnp.int32)

        @pl.when(there(dy, dz))
        def _():
            pl.semaphore_signal(barrier, inc=1, device_id=place(dy, dz), device_id_type=MESH)

    def move(slot, src, dst, dy, dz):
        copy = pltpu.make_async_remote_copy(
            src_ref=src, dst_ref=dst, send_sem=send_sem.at[slot], recv_sem=recv_sem.at[slot],
            device_id=place(dy, dz), device_id_type=MESH)
        return copy, there(dy, dz), there(-dy, -dz)

    def start(moves):
        for copy, ahead, _ in moves:
            @pl.when(ahead)
            def _():
                copy.start()

    def arrive(moves):
        for copy, _, behind in moves:
            @pl.when(behind)
            def _():
                copy.wait_recv()

    def leave(moves):
        for copy, ahead, _ in moves:
            @pl.when(ahead)
            def _():
                copy.wait_send()

    Y_WAYS = ((-1, 0, 1), (1, n - 1, 0))
    Z_WAYS = ((-1, 0, nz - 1), (1, nz - 1, 0))

    def y_moves(slot, src, dst, first):
        return [
            move(slot + i, src(first + row), dst(side), dy, 0)
            for i, (dy, row, side) in enumerate(Y_WAYS)
        ]

    def z_moves(slot, src, dst):
        return [
            move(slot + i, src(pl.ds(mine, 1)), dst(pl.ds(theirs, 1)), 0, dz)
            for i, (dz, mine, theirs) in enumerate(Z_WAYS)
        ]

    yb_moves = y_moves(0, lambda row: mag.at[:, row], lambda side: yb.at[side], 0)
    yc_moves = y_moves(2, lambda row: cot.at[:, row], lambda side: yc.at[side], 0)
    yg_moves = y_moves(4, lambda row: gE.at[:, row], lambda side: yg.at[side], 1)
    yk_moves = [
        move(
            6 + 2 * i + j, mag.at[pl.ds(1, 2), row, pl.ds(mine, 1)], yk.at[side, :, pl.ds(theirs, 1)], dy, dz
        )
        for i, (dy, row, side) in enumerate(Y_WAYS)
        for j, (dz, mine, theirs) in enumerate(Z_WAYS)
    ]
    both = pl.ds(0, 2)
    zb_moves = z_moves(10, lambda z: mag.at[both, :, z], lambda z: zb.at[:, :, z])
    zg_moves = z_moves(12, lambda z: gE.at[pl.ds(0, 3), pl.ds(1, n), z], lambda z: zg.at[:, :, z])
    zw_moves = z_moves(14, lambda z: wE.at[both, :, z], lambda z: zw.at[:, :, z])
    zh_moves = z_moves(16, lambda z: hE.at[both, pl.ds(1, n), z], lambda z: zh.at[:, :, z])

    zero = jnp.zeros((nz, nx), jnp.float32)
    for part in (0, 2):
        bE[part, 0] = zero
        bE[part, n + 1] = zero

    def wide(tile):
        return jnp.concatenate([tile] * (nx // LANES), axis=1)

    lane = lax.broadcasted_iota(jnp.int32, (nz, LANES), 1)
    sub = wide(lax.broadcasted_iota(jnp.int32, (nz, LANES), 0))
    flag = jnp.where(
        sub == nz - 1, has_high.astype(jnp.int32), jnp.where(sub == 0, has_low.astype(jnp.int32), 0)
    )
    active = flag > 0
    sign = jnp.where(sub == 0, -1.0, 1.0)

    def rim(halo):
        return jnp.where(active, sign * halo, 0.0)

    square = (
        lax.broadcasted_iota(jnp.int32, (nz, nz), 0) == lax.broadcasted_iota(jnp.int32, (nz, nz), 1)
    )
    rate_load.wait()
    r = jnp.sum(jnp.where(square, jnp.broadcast_to(rate_row[...], (nz, nz)), 0.0), axis=1, keepdims=True)
    r = jnp.broadcast_to(r, (nz, LANES))
    one = jnp.ones((nz, LANES), jnp.float32)

    r_inv = 1.0 / r
    whole, grown = one, one
    sizes = [one]
    for k in range(n):
        grown = grown + r_inv * whole
        whole = whole + grown
        sizes.append(whole)
    full_inv = 1.0 / whole
    for k in range(n):
        m = sizes[k] / sizes[k + 1]
        m_tab[k] = m
        inv_tab[k] = m * r_inv
        al_tab[n - 1 - k] = sizes[k] * full_inv
    aa, cc = sizes[n - 1] * full_inv, full_inv

    def reach(k, s):
        s_tab[k] = s
        den = cc / (1.0 - s * aa)
        den_tab[k] = den
        return aa + cc * s * den

    lax.fori_loop(0, groups, reach, jnp.zeros((nz, LANES), jnp.float32), unroll=groups <= 8)
    s_low, s_high = s_tab[me], s_tab[groups - 1 - me]
    from_low, from_high = den_tab[me] * s_low, den_tab[groups - 1 - me] * s_high
    for k in range(n):
        near, far = al_tab[k] * r_inv, al_tab[n - 1 - k] * r_inv
        w_tab[0, k] = far + from_low * near
        w_tab[1, k] = near + from_high * far

    def gather(slot):
        copies = []
        for k in range(1, groups):
            partner = lax.rem(me + k, groups)
            copies.append(pltpu.make_async_remote_copy(
                src_ref=sums.at[slot, (partner < me).astype(jnp.int32)], dst_ref=ends.at[slot, k - 1],
                send_sem=gs_sem.at[slot, k - 1], recv_sem=gr_sem.at[slot, k - 1],
                device_id={"gy": partner, "gz": lay}, device_id_type=MESH,
            ))
        return copies

    nothing = (zero,) * 6

    def collect(totals, k, rows):
        toward = (wide(w_tab[0, k]), wide(w_tab[1, k]))
        return tuple(totals[3 * way + c] + toward[way] * rows[c] for way in range(2) for c in range(3))

    def put_sums(slot, totals):
        for way in range(2):
            for c in range(3):
                sums[slot, way, c] = totals[3 * way + c]

    loads[0].wait()
    totals = nothing
    for k in range(n):
        totals = collect(totals, k, [wE[c, k + 1] for c in range(3)])
    put_sums(0, totals)

    pl.semaphore_wait(barrier, count)
    start(zb_moves)
    for copy in gather(0):
        copy.start()
    start(yb_moves)
    start(yk_moves)
    start(yc_moves)

    def slope_x(f):
        tiles = [f[:, at:at + LANES] for at in range(0, nx, LANES)]
        ahead = [pltpu.roll(tile, LANES - 1, 1) for tile in tiles] + [jnp.zeros_like(tiles[0])]
        behind = [jnp.zeros_like(tiles[0])] + [pltpu.roll(tile, 1, 1) for tile in tiles]
        return jnp.concatenate(
            [
                jnp.where(lane == LANES - 1, ahead[t + 1], ahead[t])
                - jnp.where(lane == 0, behind[t], behind[t + 1])
                for t in range(len(tiles))
            ],
            axis=1,
        )

    def slope_z(f):
        ahead = jnp.where(sub == nz - 1, 0.0, pltpu.roll(f, nz - 1, 0))
        behind = jnp.where(sub == 0, 0.0, pltpu.roll(f, 1, 0))
        return ahead - behind

    def curl(field, y, extra=None, comps=(0, 1, 2)):
        f = [field[c, y + 1] for c in comps]
        dy_x = field[comps[0], y + 2] - field[comps[0], y]
        dy_z = field[comps[2], y + 2] - field[comps[2], y]
        dz_x, dz_y = slope_z(f[0]), slope_z(f[1])
        if extra is not None:
            dz_x, dz_y = dz_x + extra[0], dz_y + extra[1]
        return (dy_z - dz_y, dz_x - slope_x(f[2]), slope_x(f[1]) - dy_x), f

    def each_row(body):
        for y in range(n):
            body(y)

    for load in loads[1:]:
        load.wait()

    def argument(y):
        turn, b = curl(bE, y)
        s = [v[c, y] for c in range(3)]
        sp = gE[SPREAD, y + 1] * (0.5 - 0.5 * (1.0 - iron_factor) * iron[y].astype(jnp.float32))
        gE[0, y + 1] = s[1] * b[2] - s[2] * b[1] - sp * turn[0]
        gE[1, y + 1] = s[2] * b[0] - s[0] * b[2] - sp * turn[1]
        gE[SPREAD, y + 1] = sp
        gE[3, y + 1] = s[0] * b[1] - s[1] * b[0] - sp * turn[2]

    each_row(argument)
    start(zg_moves)
    start(yg_moves)

    def local_solve(field, offset):
        def down(k, held):
            m = wide(m_tab[jnp.maximum(k - 1, 0)])
            rows = tuple(field[c, offset + k] + m * held[c] for c in range(3))
            for c in range(3):
                field[c, offset + k] = rows[c]
            return rows

        lax.fori_loop(0, n, down, (zero, zero, zero), unroll=True)

        def up(step, held):
            k = n - 1 - step
            m, inv = wide(m_tab[k]), wide(inv_tab[k])
            rows = tuple(field[c, offset + k] * inv + m * held[c] for c in range(3))
            for c in range(3):
                field[c, offset + k] = rows[c]
            return rows

        lax.fori_loop(0, n, up, (zero, zero, zero), unroll=True)

    left_gap, right_gap = 1.0 - s_low * aa, 1.0 - s_high * aa
    det = 1.0 / (left_gap * right_gap - s_low * s_high * cc * cc)
    ll, lr = right_gap * det, s_low * cc * det
    rr, rl = left_gap * det, s_high * cc * det
    mix[0] = ll * s_low
    mix[1] = lr * s_high
    mix[2] = rl * s_low
    mix[3] = rr * s_high
    low = one
    for k in range(1, groups):
        @pl.when(k <= me)
        def _(low=low):
            coef[0, k - 1] = ll * low
            coef[1, k - 1] = rl * low

        low = low * den_tab[jnp.maximum(me - k, 0)]
    high = one
    for k in range(1, groups):
        @pl.when(k <= groups - 1 - me)
        def _(high=high):
            coef[0, groups - k - 1] = lr * high
            coef[1, groups - k - 1] = rr * high

        high = high * den_tab[jnp.maximum(groups - 1 - me - k, 0)]

    local_solve(wE, 1)

    def gather_wait(slot):
        for copy in gather(slot):
            copy.wait_recv()

    def interface(slot, field, offset):
        first = [field[c, offset] for c in range(3)]
        last = [field[c, offset + n - 1] for c in range(3)]
        lefts, rights = [], []
        for c in range(3):
            left = wide(mix[0]) * first[c] + wide(mix[1]) * last[c]
            right = wide(mix[2]) * first[c] + wide(mix[3]) * last[c]
            for k in range(groups - 1):
                end = ends[slot, k, c]
                left = left + wide(coef[0, k]) * end
                right = right + wide(coef[1, k]) * end
            lefts.append(left)
            rights.append(right)
        return lefts, rights

    gather_wait(0)
    lefts, rights = interface(0, wE, 1)
    for c in range(3):
        wE[c, 0] = lefts[c]
        wE[c, n + 1] = rights[c]

    def relax(y):
        near, far = wide(al_tab[y]), wide(al_tab[n - 1 - y])
        for c in range(3):
            wE[c, y + 1] = wE[c, y + 1] + near * wE[c, 0] + far * wE[c, n + 1]

    each_row(relax)
    start(zw_moves)

    def pull(y):
        turn, w = curl(wE, y)
        s = [v[c, y] for c in range(3)]
        sp = gE[SPREAD, y + 1]
        adj[0, y] = w[0] + half * (turn[1] * s[2] - turn[2] * s[1])
        adj[1, y] = w[1] + half * (turn[2] * s[0] - turn[0] * s[2])
        adj[2, y] = w[2] + half * (turn[0] * s[1] - turn[1] * s[0])
        for c in range(3):
            hE[c, y + 1] = sp * turn[c]

    each_row(pull)
    start(zh_moves)

    arrive(zb_moves + yb_moves + yk_moves + yg_moves + zg_moves)
    leave(yg_moves + zg_moves)

    for side, way in SIDES:
        have = (has_left, has_right)[side]
        edge, halo, y = (1, 0, 0) if side == 0 else (n, n + 1, n - 1)
        beyond, sp = way * yg[side, SPREAD], way * gE[SPREAD, edge]
        g_x = yg[side, 0] + beyond * (bE[2, edge] + way * rim(yk[side, 0]))
        g_z = yg[side, 3] - beyond * bE[0, edge]
        gE[0, halo] = jnp.where(have, g_x, 0.0)
        gE[3, halo] = jnp.where(have, g_z, 0.0)
        gE[0, edge] = gE[0, edge] - jnp.where(have, sp * yb[side, 2], 0.0)
        gE[3, edge] = gE[3, edge] + jnp.where(have, sp * yb[side, 0], 0.0)
        zg[0, y] = zg[0, y] - jnp.where(have, way * zg[SPREAD, y] * yk[side, 1], 0.0)

    def mend_argument(y):
        sp = gE[SPREAD, y + 1]
        gE[0, y + 1] = gE[0, y + 1] + sp * rim(zb[1, y])
        gE[1, y + 1] = gE[1, y + 1] - sp * rim(zb[0, y])

    each_row(mend_argument)

    totals = nothing
    for y in range(n):
        b = [bE[c, y + 1] for c in range(3)]
        sp = zg[SPREAD, y]
        extra = (
            jnp.where(active, sign * zg[0, y] - sp * b[1], 0.0),
            jnp.where(active, sign * zg[1, y] + sp * b[0], 0.0),
        )
        turn, _ = curl(gE, y, extra, G_COMPS)
        rows = [b[c] + half * turn[c] for c in range(3)]
        for c in range(3):
            new[c, y] = rows[c]
        totals = collect(totals, y, rows)
    put_sums(1, totals)
    for copy in gather(1):
        copy.start()

    arrive(yc_moves)
    wide_inv = wide(r_inv)
    for side, way in SIDES:
        have = (has_left, has_right)[side]
        edge, halo = (1, 0) if side == 0 else (n, n + 1)
        sp = yg[side, SPREAD]
        slope = {}
        for c in (0, 2):
            near, rim_row = wE[c, edge], wE[c, halo]
            outer = rim_row + (rim_row - near) + wide_inv * (rim_row - yc[side, c])
            slope[c] = way * (outer - near)
        cross = wE[1, halo]
        hE[0, halo] = jnp.where(have, sp * (slope[2] - slope_z(cross)), 0.0)
        hE[2, halo] = jnp.where(have, sp * (slope_x(cross) - slope[0]), 0.0)

    local_solve(new, 0)
    arrive(zw_moves + zh_moves)
    leave(zh_moves)

    for side, way in SIDES:
        have = (has_left, has_right)[side]
        halo = 0 if side == 0 else n + 1
        hE[0, halo] = hE[0, halo] - jnp.where(have, yg[side, SPREAD] * rim(zw[1, halo]), 0.0)

    def mend_pull(y):
        c_x, c_y = rim(zw[0, y + 1]), rim(zw[1, y + 1])
        sp = gE[SPREAD, y + 1]
        s = [v[c, y] for c in range(3)]
        hE[0, y + 1] = hE[0, y + 1] - sp * c_y
        hE[1, y + 1] = hE[1, y + 1] + sp * c_x
        h_x, h_y = half * c_x, half * c_y
        adj[0, y] = adj[0, y] + h_x * s[2]
        adj[1, y] = adj[1, y] + h_y * s[2]
        adj[2, y] = adj[2, y] - (h_y * s[1] + h_x * s[0])

    each_row(mend_pull)

    def finish_adjoint(y):
        sp = zg[SPREAD, y]
        extra = (
            jnp.where(active, sign * zh[0, y] + sp * wE[1, y + 1], 0.0),
            jnp.where(active, sign * zh[1, y] - sp * wE[0, y + 1], 0.0),
        )
        turn, _ = curl(hE, y, extra)
        for c in range(3):
            adj[c, y] = adj[c, y] - half * turn[c]

    each_row(finish_adjoint)

    gather_wait(1)
    lefts, rights = interface(1, new, 0)

    def finish(y):
        near, far = wide(al_tab[y]), wide(al_tab[n - 1 - y])
        for c in range(3):
            new[c, y] = new[c, y] + near * lefts[c] + far * rights[c]

    each_row(finish)

    leave(yb_moves + yc_moves + yk_moves + zb_moves + zw_moves)
    for slot in range(2):
        for copy in gather(slot):
            copy.wait_send()


def hand_over(new, adj, new_out, adj_out, sem):
    copies = [
        pltpu.make_async_copy(new, new_out, sem.at[0]),
        pltpu.make_async_copy(adj, adj_out, sem.at[1]),
    ]
    for copy in copies:
        copy.start()
    for copy in copies:
        copy.wait()


def local(groups, layers, magnetic, velocity, diffusivity, material, plane_rate, cotangent):
    _, n, nz, nx = magnetic.shape
    block = (3, n, nz, nx)
    rimmed = (3, n + 2, nz, nx)
    f32 = jnp.float32
    anywhere = pl.BlockSpec(memory_space=pl.ANY)
    inside = pl.BlockSpec(memory_space=pltpu.VMEM)
    args = [
        pltpu.with_memory_space_constraint(array, pltpu.HBM)
        for array in (magnetic, velocity, diffusivity, material, plane_rate.reshape(1, nz), cotangent)
    ]
    new, adj = pl.pallas_call(
        functools.partial(kernel, groups, layers, n),
        out_shape=[jax.ShapeDtypeStruct(block, f32)] * 2,
        in_specs=[anywhere] * 6,
        out_specs=[inside] * 2,
        scratch_shapes=[
            pltpu.VMEM(rimmed, f32),
            pltpu.VMEM((4, n + 2, nz, nx), f32),
            pltpu.VMEM(rimmed, f32),
            pltpu.VMEM(rimmed, f32),
            pltpu.VMEM(block, f32),
            pltpu.VMEM((n, nz, nx), jnp.int32),
            pltpu.VMEM((1, nz), f32),
            pltpu.VMEM((2, n, nz, nx), f32),
            pltpu.VMEM((3, n, nz, nx), f32),
            pltpu.VMEM((2, n + 2, nz, nx), f32),
            pltpu.VMEM((2, n, nz, nx), f32),
            pltpu.VMEM((2, 3, nz, nx), f32),
            pltpu.VMEM((2, 3, nz, nx), f32),
            pltpu.VMEM((2, 4, nz, nx), f32),
            pltpu.VMEM((2, 2, nz, nx), f32),
            pltpu.VMEM((2, groups - 1, 3, nz, nx), f32),
            pltpu.VMEM((2, 2, 3, nz, nx), f32),
            pltpu.VMEM((n, nz, LANES), f32),
            pltpu.VMEM((n, nz, LANES), f32),
            pltpu.VMEM((n, nz, LANES), f32),
            pltpu.VMEM((groups, nz, LANES), f32),
            pltpu.VMEM((groups, nz, LANES), f32),
            pltpu.VMEM((2, n, nz, LANES), f32),
            pltpu.VMEM((4, nz, LANES), f32),
            pltpu.VMEM((2, groups - 1, nz, LANES), f32),
            pltpu.SemaphoreType.DMA((6,)),
            pltpu.SemaphoreType.DMA((N_MOVES,)),
            pltpu.SemaphoreType.DMA((N_MOVES,)),
            pltpu.SemaphoreType.DMA((2, groups - 1)),
            pltpu.SemaphoreType.DMA((2, groups - 1)),
        ],
        compiler_params=pltpu.CompilerParams(
            collective_id=0, has_side_effects=True, vmem_limit_bytes=24 * 2**20
        ),
    )(*args)
    return tuple(pl.pallas_call(
        hand_over,
        out_shape=[jax.ShapeDtypeStruct(block, f32)] * 2,
        in_specs=[anywhere] * 2,
        out_specs=[anywhere] * 2,
        scratch_shapes=[pltpu.SemaphoreType.DMA((2,))],
        compiler_params=pltpu.CompilerParams(vmem_limit_bytes=2**20),
    )(new, adj))


def solution(mesh):
    in_specs = (
        P(None, "gy", "gz", None),
        P(None, "gy", "gz", None),
        P("gy", "gz", None),
        P("gy", "gz", None),
        P("gz"),
        P(None, "gy", "gz", None),
    )
    out_specs = (P(None, "gy", "gz", None), P(None, "gy", "gz", None))
    body = functools.partial(local, mesh.shape["gy"], mesh.shape["gz"])
    return jax.shard_map(body, mesh=mesh, in_specs=in_specs, out_specs=out_specs, check_vma=False)
```

```python
import functools
import jax
import jax.numpy as jnp
from jax import lax
from jax.experimental import pallas as pl
from jax.experimental.pallas import tpu as pltpu
from jax.sharding import PartitionSpec as P

step_size = 0.1
iron_factor = 0.2
MESH = pl.DeviceIdType.MESH
LANES = 128
SIDES = ((0, -1), (1, 1))
N_WAYS = 10
G_COMPS = (0, 1, 3)
SPREAD = 2


def kernel(
    groups, layers, n, mag, vel, dif, mat, rate, cot, new, adj,
    bE, gE, wE, hE, v, iron, rate_row, z_one, z_two, y_one, yk, ends, sums,
    m_tab, inv_tab, al_tab, s_tab, den_tab, w_tab, mix, coef,
    load_sem, send_sem, recv_sem, gs_sem, gr_sem,
):
    me = lax.axis_index("gy")
    lay = lax.axis_index("gz")
    nx = bE.shape[-1]
    nz = bE.shape[-2]
    half = 0.5 * step_size

    rate_load = pltpu.make_async_copy(rate, rate_row, load_sem.at[4])
    rate_load.start()
    loads = [
        pltpu.make_async_copy(cot, wE.at[:, pl.ds(1, n)], load_sem.at[1]),
        pltpu.make_async_copy(mag, bE.at[:, pl.ds(1, n)], load_sem.at[0]),
        pltpu.make_async_copy(dif, gE.at[SPREAD, pl.ds(1, n)], load_sem.at[3]),
        pltpu.make_async_copy(mat, iron, load_sem.at[3]),
        pltpu.make_async_copy(vel, v, load_sem.at[2]),
    ]
    for load in loads:
        load.start()

    has_left, has_right = me > 0, me < groups - 1
    has_low, has_high = lay > 0, lay < layers - 1

    def there(dy, dz):
        found = None
        for step, low, high in ((dy, has_left, has_right), (dz, has_low, has_high)):
            if step:
                seen = low if step < 0 else high
                found = seen if found is None else jnp.logical_and(found, seen)
        return found

    def place(dy, dz):
        return {
            "gy": jnp.clip(me + dy, 0, groups - 1) if dy else me,
            "gz": jnp.clip(lay + dz, 0, layers - 1) if dz else lay,
        }

    around = [(dy, dz) for dy in (-1, 0, 1) for dz in (-1, 0, 1) if dz]
    barrier = pltpu.get_barrier_semaphore()
    for k in range(1, groups):
        pl.semaphore_signal(
            barrier, inc=1, device_id={"gy": lax.rem(me + k, groups), "gz": lay}, device_id_type=MESH
        )
    count = jnp.int32(groups - 1)
    for dy, dz in around:
        count = count + there(dy, dz).astype(jnp.int32)

        @pl.when(there(dy, dz))
        def _():
            pl.semaphore_signal(barrier, inc=1, device_id=place(dy, dz), device_id_type=MESH)

    def move(slot, src, dst, dy, dz):
        copy = pltpu.make_async_remote_copy(
            src_ref=src, dst_ref=dst, send_sem=send_sem.at[slot], recv_sem=recv_sem.at[slot],
            device_id=place(dy, dz), device_id_type=MESH)
        return copy, there(dy, dz), there(-dy, -dz)

    def start(moves):
        for copy, ahead, _ in moves:
            @pl.when(ahead)
            def _():
                copy.start()

    def arrive(moves):
        for copy, _, behind in moves:
            @pl.when(behind)
            def _():
                copy.wait_recv()

    def leave(moves):
        for copy, ahead, _ in moves:
            @pl.when(ahead)
            def _():
                copy.wait_send()

    Y_WAYS = ((-1, 0, 1), (1, n - 1, 0))
    Z_WAYS = ((-1, 0, nz - 1), (1, nz - 1, 0))

    def y_moves(slot, src, dst, first):
        return [
            move(slot + i, src(first + row), dst(side), dy, 0)
            for i, (dy, row, side) in enumerate(Y_WAYS)
        ]

    def z_moves(slot, src, dst):
        return [
            move(slot + i, src(pl.ds(mine, 1)), dst(pl.ds(theirs, 1)), 0, dz)
            for i, (dz, mine, theirs) in enumerate(Z_WAYS)
        ]

    b_rows, c_rows, g_rows = pl.ds(0, 3), pl.ds(3, 3), pl.ds(6, 4)
    yb_moves = y_moves(0, lambda row: mag.at[:, row], lambda side: y_one.at[side, b_rows], 0)
    yc_moves = y_moves(0, lambda row: cot.at[:, row], lambda side: y_one.at[side, c_rows], 0)
    yg_moves = y_moves(0, lambda row: gE.at[:, row], lambda side: y_one.at[side, g_rows], 1)
    y_all = [
        move(i, y_one.at[side], y_one.at[side], dy, 0) for i, (dy, _, side) in enumerate(Y_WAYS)
    ]
    yk_moves = [
        move(
            6 + 2 * i + j, mag.at[pl.ds(1, 2), row, pl.ds(mine, 1)], yk.at[side, :, pl.ds(theirs, 1)], dy, dz
        )
        for i, (dy, row, side) in enumerate(Y_WAYS)
        for j, (dz, mine, theirs) in enumerate(Z_WAYS)
    ]
    both = pl.ds(0, 2)
    w_rows, h_rows = pl.ds(0, n + 2), pl.ds(n + 2, n)
    zb_moves = z_moves(2, lambda z: mag.at[both, :, z], lambda z: z_one.at[both, :, z])
    zg_moves = z_moves(2, lambda z: gE.at[pl.ds(0, 3), pl.ds(1, n), z], lambda z: z_one.at[pl.ds(2, 3), :, z])
    z_one_all = [
        move(2 + i, z_one.at[:, :, pl.ds(theirs, 1)], z_one.at[:, :, pl.ds(theirs, 1)], 0, dz)
        for i, (dz, _, theirs) in enumerate(Z_WAYS)
    ]
    zw_moves = z_moves(4, lambda z: wE.at[both, :, z], lambda z: z_two.at[:, w_rows, z])
    zh_moves = z_moves(4, lambda z: hE.at[both, pl.ds(1, n), z], lambda z: z_two.at[:, h_rows, z])
    z_two_all = [
        move(4 + i, z_two.at[:, :, pl.ds(theirs, 1)], z_two.at[:, :, pl.ds(theirs, 1)], 0, dz)
        for i, (dz, _, theirs) in enumerate(Z_WAYS)
    ]

    zero = jnp.zeros((nz, nx), jnp.float32)
    for part in (0, 2):
        bE[part, 0] = zero
        bE[part, n + 1] = zero

    def wide(tile):
        return jnp.concatenate([tile] * (nx // LANES), axis=1)

    lane = lax.broadcasted_iota(jnp.int32, (nz, LANES), 1)
    sub = wide(lax.broadcasted_iota(jnp.int32, (nz, LANES), 0))
    flag = jnp.where(
        sub == nz - 1, has_high.astype(jnp.int32), jnp.where(sub == 0, has_low.astype(jnp.int32), 0)
    )
    active = flag > 0
    sign = jnp.where(sub == 0, -1.0, 1.0)

    def rim(halo):
        return jnp.where(active, sign * halo, 0.0)

    square = (
        lax.broadcasted_iota(jnp.int32, (nz, nz), 0) == lax.broadcasted_iota(jnp.int32, (nz, nz), 1)
    )
    rate_load.wait()
    r = jnp.sum(jnp.where(square, jnp.broadcast_to(rate_row[...], (nz, nz)), 0.0), axis=1, keepdims=True)
    r = jnp.broadcast_to(r, (nz, LANES))
    one = jnp.ones((nz, LANES), jnp.float32)

    r_inv = 1.0 / r
    whole, grown = one, one
    sizes = [one]
    for k in range(n):
        grown = grown + r_inv * whole
        whole = whole + grown
        sizes.append(whole)
    full_inv = 1.0 / whole
    for k in range(n):
        m = sizes[k] / sizes[k + 1]
        m_tab[k] = m
        inv_tab[k] = m * r_inv
        al_tab[n - 1 - k] = sizes[k] * full_inv
    aa, cc = sizes[n - 1] * full_inv, full_inv

    def reach(k, s):
        s_tab[k] = s
        den = cc / (1.0 - s * aa)
        den_tab[k] = den
        return aa + cc * s * den

    lax.fori_loop(0, groups, reach, jnp.zeros((nz, LANES), jnp.float32), unroll=groups <= 8)
    s_low, s_high = s_tab[me], s_tab[groups - 1 - me]
    from_low, from_high = den_tab[me] * s_low, den_tab[groups - 1 - me] * s_high
    for k in range(n):
        near, far = al_tab[k] * r_inv, al_tab[n - 1 - k] * r_inv
        w_tab[0, k] = far + from_low * near
        w_tab[1, k] = near + from_high * far

    def gather(slot):
        copies = []
        for k in range(1, groups):
            partner = lax.rem(me + k, groups)
            copies.append(pltpu.make_async_remote_copy(
                src_ref=sums.at[slot, (partner < me).astype(jnp.int32)], dst_ref=ends.at[slot, k - 1],
                send_sem=gs_sem.at[slot], recv_sem=gr_sem.at[slot],
                device_id={"gy": partner, "gz": lay}, device_id_type=MESH,
            ))
        return copies

    def gather_all(slot):
        return pltpu.make_async_remote_copy(
            src_ref=ends.at[slot], dst_ref=ends.at[slot], send_sem=gs_sem.at[slot], recv_sem=gr_sem.at[slot],
            device_id={"gy": lax.rem(me + 1, groups), "gz": lay}, device_id_type=MESH)

    nothing = (zero,) * 6

    def collect(totals, k, rows):
        toward = (wide(w_tab[0, k]), wide(w_tab[1, k]))
        return tuple(totals[3 * way + c] + toward[way] * rows[c] for way in range(2) for c in range(3))

    def put_sums(slot, totals):
        for way in range(2):
            for c in range(3):
                sums[slot, way, c] = totals[3 * way + c]

    loads[0].wait()
    totals = nothing
    for k in range(n):
        totals = collect(totals, k, [wE[c, k + 1] for c in range(3)])
    put_sums(0, totals)

    pl.semaphore_wait(barrier, count)
    start(zb_moves)
    for copy in gather(0):
        copy.start()
    start(yb_moves)
    start(yk_moves)
    start(yc_moves)

    def slope_x(f):
        tiles = [f[:, at:at + LANES] for at in range(0, nx, LANES)]
        ahead = [pltpu.roll(tile, LANES - 1, 1) for tile in tiles] + [jnp.zeros_like(tiles[0])]
        behind = [jnp.zeros_like(tiles[0])] + [pltpu.roll(tile, 1, 1) for tile in tiles]
        return jnp.concatenate(
            [
                jnp.where(lane == LANES - 1, ahead[t + 1], ahead[t])
                - jnp.where(lane == 0, behind[t], behind[t + 1])
                for t in range(len(tiles))
            ],
            axis=1,
        )

    def slope_z(f):
        ahead = jnp.where(sub == nz - 1, 0.0, pltpu.roll(f, nz - 1, 0))
        behind = jnp.where(sub == 0, 0.0, pltpu.roll(f, 1, 0))
        return ahead - behind

    def curl(field, y, extra=None, comps=(0, 1, 2)):
        f = [field[c, y + 1] for c in comps]
        dy_x = field[comps[0], y + 2] - field[comps[0], y]
        dy_z = field[comps[2], y + 2] - field[comps[2], y]
        dz_x, dz_y = slope_z(f[0]), slope_z(f[1])
        if extra is not None:
            dz_x, dz_y = dz_x + extra[0], dz_y + extra[1]
        return (dy_z - dz_y, dz_x - slope_x(f[2]), slope_x(f[1]) - dy_x), f

    def each_row(body):
        for y in range(n):
            body(y)

    loads[1].wait()
    pltpu.make_async_copy(z_one.at[pl.ds(0, 2)], z_one.at[pl.ds(2, 2)], load_sem.at[3]).wait()
    loads[4].wait()

    def argument(y):
        turn, b = curl(bE, y)
        s = [v[c, y] for c in range(3)]
        sp = gE[SPREAD, y + 1] * (0.5 - 0.5 * (1.0 - iron_factor) * iron[y].astype(jnp.float32))
        gE[0, y + 1] = s[1] * b[2] - s[2] * b[1] - sp * turn[0]
        gE[1, y + 1] = s[2] * b[0] - s[0] * b[2] - sp * turn[1]
        gE[SPREAD, y + 1] = sp
        gE[3, y + 1] = s[0] * b[1] - s[1] * b[0] - sp * turn[2]

    each_row(argument)
    start(zg_moves)
    start(yg_moves)

    def local_solve(field, offset):
        def down(k, held):
            m = wide(m_tab[jnp.maximum(k - 1, 0)])
            rows = tuple(field[c, offset + k] + m * held[c] for c in range(3))
            for c in range(3):
                field[c, offset + k] = rows[c]
            return rows

        lax.fori_loop(0, n, down, (zero, zero, zero), unroll=True)

        def up(step, held):
            k = n - 1 - step
            m, inv = wide(m_tab[k]), wide(inv_tab[k])
            rows = tuple(field[c, offset + k] * inv + m * held[c] for c in range(3))
            for c in range(3):
                field[c, offset + k] = rows[c]
            return rows

        lax.fori_loop(0, n, up, (zero, zero, zero), unroll=True)

    left_gap, right_gap = 1.0 - s_low * aa, 1.0 - s_high * aa
    det = 1.0 / (left_gap * right_gap - s_low * s_high * cc * cc)
    ll, lr = right_gap * det, s_low * cc * det
    rr, rl = left_gap * det, s_high * cc * det
    mix[0] = ll * s_low
    mix[1] = lr * s_high
    mix[2] = rl * s_low
    mix[3] = rr * s_high
    low = one
    for k in range(1, groups):
        @pl.when(k <= me)
        def _(low=low):
            coef[0, k - 1] = ll * low
            coef[1, k - 1] = rl * low

        low = low * den_tab[jnp.maximum(me - k, 0)]
    high = one
    for k in range(1, groups):
        @pl.when(k <= groups - 1 - me)
        def _(high=high):
            coef[0, groups - k - 1] = lr * high
            coef[1, groups - k - 1] = rr * high

        high = high * den_tab[jnp.maximum(groups - 1 - me - k, 0)]

    local_solve(wE, 1)

    def interface(slot, field, offset):
        first = [field[c, offset] for c in range(3)]
        last = [field[c, offset + n - 1] for c in range(3)]
        lefts, rights = [], []
        for c in range(3):
            left = wide(mix[0]) * first[c] + wide(mix[1]) * last[c]
            right = wide(mix[2]) * first[c] + wide(mix[3]) * last[c]
            for k in range(groups - 1):
                end = ends[slot, k, c]
                left = left + wide(coef[0, k]) * end
                right = right + wide(coef[1, k]) * end
            lefts.append(left)
            rights.append(right)
        return lefts, rights

    gather_all(0).wait_recv()
    lefts, rights = interface(0, wE, 1)
    for c in range(3):
        wE[c, 0] = lefts[c]
        wE[c, n + 1] = rights[c]

    def relax(y):
        near, far = wide(al_tab[y]), wide(al_tab[n - 1 - y])
        for c in range(3):
            wE[c, y + 1] = wE[c, y + 1] + near * wE[c, 0] + far * wE[c, n + 1]

    each_row(relax)
    start(zw_moves)

    def pull(y):
        turn, w = curl(wE, y)
        s = [v[c, y] for c in range(3)]
        sp = gE[SPREAD, y + 1]
        adj[0, y] = w[0] + half * (turn[1] * s[2] - turn[2] * s[1])
        adj[1, y] = w[1] + half * (turn[2] * s[0] - turn[0] * s[2])
        adj[2, y] = w[2] + half * (turn[0] * s[1] - turn[1] * s[0])
        for c in range(3):
            hE[c, y + 1] = sp * turn[c]

    each_row(pull)
    start(zh_moves)

    arrive(y_all + yk_moves + z_one_all)
    leave(y_all + z_one_all)

    for side, way in SIDES:
        have = (has_left, has_right)[side]
        edge, halo, y = (1, 0, 0) if side == 0 else (n, n + 1, n - 1)
        beyond, sp = way * y_one[side, 6 + SPREAD], way * gE[SPREAD, edge]
        g_x = y_one[side, 6] + beyond * (bE[2, edge] + way * rim(yk[side, 0]))
        g_z = y_one[side, 9] - beyond * bE[0, edge]
        gE[0, halo] = jnp.where(have, g_x, 0.0)
        gE[3, halo] = jnp.where(have, g_z, 0.0)
        gE[0, edge] = gE[0, edge] - jnp.where(have, sp * y_one[side, 2], 0.0)
        gE[3, edge] = gE[3, edge] + jnp.where(have, sp * y_one[side, 0], 0.0)
        z_one[2, y] = z_one[2, y] - jnp.where(have, way * z_one[2 + SPREAD, y] * yk[side, 1], 0.0)

    def mend_argument(y):
        sp = gE[SPREAD, y + 1]
        gE[0, y + 1] = gE[0, y + 1] + sp * rim(z_one[1, y])
        gE[1, y + 1] = gE[1, y + 1] - sp * rim(z_one[0, y])

    each_row(mend_argument)

    totals = nothing
    for y in range(n):
        b = [bE[c, y + 1] for c in range(3)]
        sp = z_one[2 + SPREAD, y]
        extra = (
            jnp.where(active, sign * z_one[2, y] - sp * b[1], 0.0),
            jnp.where(active, sign * z_one[3, y] + sp * b[0], 0.0),
        )
        turn, _ = curl(gE, y, extra, G_COMPS)
        rows = [b[c] + half * turn[c] for c in range(3)]
        for c in range(3):
            new[c, y] = rows[c]
        totals = collect(totals, y, rows)
    put_sums(1, totals)
    for copy in gather(1):
        copy.start()

    wide_inv = wide(r_inv)
    for side, way in SIDES:
        have = (has_left, has_right)[side]
        edge, halo = (1, 0) if side == 0 else (n, n + 1)
        sp = y_one[side, 6 + SPREAD]
        slope = {}
        for c in (0, 2):
            near, rim_row = wE[c, edge], wE[c, halo]
            outer = rim_row + (rim_row - near) + wide_inv * (rim_row - y_one[side, 3 + c])
            slope[c] = way * (outer - near)
        cross = wE[1, halo]
        hE[0, halo] = jnp.where(have, sp * (slope[2] - slope_z(cross)), 0.0)
        hE[2, halo] = jnp.where(have, sp * (slope_x(cross) - slope[0]), 0.0)

    local_solve(new, 0)
    arrive(z_two_all)
    leave(z_two_all)

    for side, way in SIDES:
        have = (has_left, has_right)[side]
        halo = 0 if side == 0 else n + 1
        hE[0, halo] = hE[0, halo] - jnp.where(have, y_one[side, 6 + SPREAD] * rim(z_two[1, halo]), 0.0)

    def mend_pull(y):
        c_x, c_y = rim(z_two[0, y + 1]), rim(z_two[1, y + 1])
        sp = gE[SPREAD, y + 1]
        s = [v[c, y] for c in range(3)]
        hE[0, y + 1] = hE[0, y + 1] - sp * c_y
        hE[1, y + 1] = hE[1, y + 1] + sp * c_x
        h_x, h_y = half * c_x, half * c_y
        adj[0, y] = adj[0, y] + h_x * s[2]
        adj[1, y] = adj[1, y] + h_y * s[2]
        adj[2, y] = adj[2, y] - (h_y * s[1] + h_x * s[0])

    each_row(mend_pull)

    def finish_adjoint(y):
        sp = z_one[2 + SPREAD, y]
        extra = (
            jnp.where(active, sign * z_two[0, n + 2 + y] + sp * wE[1, y + 1], 0.0),
            jnp.where(active, sign * z_two[1, n + 2 + y] - sp * wE[0, y + 1], 0.0),
        )
        turn, _ = curl(hE, y, extra)
        for c in range(3):
            adj[c, y] = adj[c, y] - half * turn[c]

    each_row(finish_adjoint)

    gather_all(1).wait_recv()
    lefts, rights = interface(1, new, 0)

    def finish(y):
        near, far = wide(al_tab[y]), wide(al_tab[n - 1 - y])
        for c in range(3):
            new[c, y] = new[c, y] + near * lefts[c] + far * rights[c]

    each_row(finish)

    leave(yk_moves)
    for slot in range(2):
        gather_all(slot).wait_send()


def hand_over(new, adj, new_out, adj_out, sem):
    copies = [
        pltpu.make_async_copy(new, new_out, sem.at[0]),
        pltpu.make_async_copy(adj, adj_out, sem.at[1]),
    ]
    for copy in copies:
        copy.start()
    for copy in copies:
        copy.wait()


def local(groups, layers, magnetic, velocity, diffusivity, material, plane_rate, cotangent):
    _, n, nz, nx = magnetic.shape
    block = (3, n, nz, nx)
    rimmed = (3, n + 2, nz, nx)
    f32 = jnp.float32
    anywhere = pl.BlockSpec(memory_space=pl.ANY)
    inside = pl.BlockSpec(memory_space=pltpu.VMEM)
    args = [
        pltpu.with_memory_space_constraint(array, pltpu.HBM)
        for array in (magnetic, velocity, diffusivity, material, plane_rate.reshape(1, nz), cotangent)
    ]
    new, adj = pl.pallas_call(
        functools.partial(kernel, groups, layers, n),
        out_shape=[jax.ShapeDtypeStruct(block, f32)] * 2,
        in_specs=[anywhere] * 6,
        out_specs=[inside] * 2,
        scratch_shapes=[
            pltpu.VMEM(rimmed, f32),
            pltpu.VMEM((4, n + 2, nz, nx), f32),
            pltpu.VMEM(rimmed, f32),
            pltpu.VMEM(rimmed, f32),
            pltpu.VMEM(block, f32),
            pltpu.VMEM((n, nz, nx), jnp.int32),
            pltpu.VMEM((1, nz), f32),
            pltpu.VMEM((5, n, nz, nx), f32),
            pltpu.VMEM((2, 2 * n + 2, nz, nx), f32),
            pltpu.VMEM((2, 10, nz, nx), f32),
            pltpu.VMEM((2, 2, nz, nx), f32),
            pltpu.VMEM((2, groups - 1, 3, nz, nx), f32),
            pltpu.VMEM((2, 2, 3, nz, nx), f32),
            pltpu.VMEM((n, nz, LANES), f32),
            pltpu.VMEM((n, nz, LANES), f32),
            pltpu.VMEM((n, nz, LANES), f32),
            pltpu.VMEM((groups, nz, LANES), f32),
            pltpu.VMEM((groups, nz, LANES), f32),
            pltpu.VMEM((2, n, nz, LANES), f32),
            pltpu.VMEM((4, nz, LANES), f32),
            pltpu.VMEM((2, groups - 1, nz, LANES), f32),
            pltpu.SemaphoreType.DMA((5,)),
            pltpu.SemaphoreType.DMA((N_WAYS,)),
            pltpu.SemaphoreType.DMA((N_WAYS,)),
            pltpu.SemaphoreType.DMA((2,)),
            pltpu.SemaphoreType.DMA((2,)),
        ],
        compiler_params=pltpu.CompilerParams(
            collective_id=0, has_side_effects=True, vmem_limit_bytes=24 * 2**20
        ),
    )(*args)
    return tuple(pl.pallas_call(
        hand_over,
        out_shape=[jax.ShapeDtypeStruct(block, f32)] * 2,
        in_specs=[anywhere] * 2,
        out_specs=[anywhere] * 2,
        scratch_shapes=[pltpu.SemaphoreType.DMA((2,))],
        compiler_params=pltpu.CompilerParams(vmem_limit_bytes=2**20),
    )(new, adj))


def solution(mesh):
    in_specs = (
        P(None, "gy", "gz", None),
        P(None, "gy", "gz", None),
        P("gy", "gz", None),
        P("gy", "gz", None),
        P("gz"),
        P(None, "gy", "gz", None),
    )
    out_specs = (P(None, "gy", "gz", None), P(None, "gy", "gz", None))
    body = functools.partial(local, mesh.shape["gy"], mesh.shape["gz"])
    return jax.shard_map(body, mesh=mesh, in_specs=in_specs, out_specs=out_specs, check_vma=False)
```

```python
import functools
import jax
import jax.numpy as jnp
from jax import lax
from jax.experimental import pallas as pl
from jax.experimental.pallas import tpu as pltpu
from jax.sharding import PartitionSpec as P

step_size = 0.1
iron_factor = 0.2
MESH = pl.DeviceIdType.MESH
LANES = 128
SIDES = ((0, -1), (1, 1))
N_WAYS = 10
G_COMPS = (1, 0, 3)
SPREAD = 2
NEAR_SPREAD = 5


def kernel(
    groups, layers, n, mag, vel, dif, mat, rate, cot, new, adj,
    bE, gE, wE, hE, v, iron, rate_row, z_one, z_two, y_one, yk, ends, sums,
    m_tab, inv_tab, al_tab, s_tab, den_tab, w_tab, mix, coef,
    load_sem, send_sem, recv_sem, gs_sem, gr_sem,
):
    me = lax.axis_index("gy")
    lay = lax.axis_index("gz")
    nx = bE.shape[-1]
    nz = bE.shape[-2]
    half = 0.5 * step_size

    rate_load = pltpu.make_async_copy(rate, rate_row, load_sem.at[4])
    rate_load.start()
    loads = [
        pltpu.make_async_copy(cot, wE.at[:, pl.ds(1, n)], load_sem.at[1]),
        pltpu.make_async_copy(mag, bE.at[:, pl.ds(1, n)], load_sem.at[0]),
        pltpu.make_async_copy(dif, gE.at[SPREAD, pl.ds(1, n)], load_sem.at[3]),
        pltpu.make_async_copy(mat, iron, load_sem.at[3]),
        pltpu.make_async_copy(vel, v, load_sem.at[2]),
    ]
    for load in loads:
        load.start()

    has_left, has_right = me > 0, me < groups - 1
    has_low, has_high = lay > 0, lay < layers - 1

    def there(dy, dz):
        found = None
        for step, low, high in ((dy, has_left, has_right), (dz, has_low, has_high)):
            if step:
                seen = low if step < 0 else high
                found = seen if found is None else jnp.logical_and(found, seen)
        return found

    def place(dy, dz):
        return {
            "gy": jnp.clip(me + dy, 0, groups - 1) if dy else me,
            "gz": jnp.clip(lay + dz, 0, layers - 1) if dz else lay,
        }

    around = [(dy, dz) for dy in (-1, 0, 1) for dz in (-1, 0, 1) if dz]
    barrier = pltpu.get_barrier_semaphore()
    for k in range(1, groups):
        pl.semaphore_signal(
            barrier, inc=1, device_id={"gy": lax.rem(me + k, groups), "gz": lay}, device_id_type=MESH
        )
    count = jnp.int32(groups - 1)
    for dy, dz in around:
        count = count + there(dy, dz).astype(jnp.int32)

        @pl.when(there(dy, dz))
        def _():
            pl.semaphore_signal(barrier, inc=1, device_id=place(dy, dz), device_id_type=MESH)

    def move(slot, src, dst, dy, dz):
        copy = pltpu.make_async_remote_copy(
            src_ref=src, dst_ref=dst, send_sem=send_sem.at[slot], recv_sem=recv_sem.at[slot],
            device_id=place(dy, dz), device_id_type=MESH)
        return copy, there(dy, dz), there(-dy, -dz)

    def start(moves):
        for copy, ahead, _ in moves:
            @pl.when(ahead)
            def _():
                copy.start()

    def arrive(moves):
        for copy, _, behind in moves:
            @pl.when(behind)
            def _():
                copy.wait_recv()

    def leave(moves):
        for copy, ahead, _ in moves:
            @pl.when(ahead)
            def _():
                copy.wait_send()

    Y_WAYS = ((-1, 0, 1), (1, n - 1, 0))
    Z_WAYS = ((-1, 0, nz - 1), (1, nz - 1, 0))

    def y_moves(slot, src, dst, first):
        return [
            move(slot + i, src(first + row), dst(side), dy, 0)
            for i, (dy, row, side) in enumerate(Y_WAYS)
        ]

    def z_moves(slot, src, dst):
        return [
            move(slot + i, src(pl.ds(mine, 1)), dst(pl.ds(theirs, 1)), 0, dz)
            for i, (dz, mine, theirs) in enumerate(Z_WAYS)
        ]

    yb_moves = [
        copy for i, c in enumerate((0, 2))
        for copy in y_moves(0, lambda row: mag.at[c, row], lambda side: y_one.at[side, i], 0)
    ]
    yc_moves = [
        copy for i, c in enumerate((0, 2))
        for copy in y_moves(0, lambda row: cot.at[c, row], lambda side: y_one.at[side, 2 + i], 0)
    ]
    yg_moves = y_moves(0, lambda row: gE.at[pl.ds(1, 3), row], lambda side: y_one.at[side, pl.ds(4, 3)], 1)
    y_all = [
        move(i, y_one.at[side], y_one.at[side], dy, 0) for i, (dy, _, side) in enumerate(Y_WAYS)
    ]
    yk_moves = [
        move(
            6 + 2 * i + j, mag.at[pl.ds(1, 2), row, pl.ds(mine, 1)], yk.at[side, :, pl.ds(theirs, 1)], dy, dz
        )
        for i, (dy, row, side) in enumerate(Y_WAYS)
        for j, (dz, mine, theirs) in enumerate(Z_WAYS)
    ]
    both = pl.ds(0, 2)
    w_rows, h_rows = pl.ds(0, n + 2), pl.ds(n + 2, n)
    zb_moves = z_moves(2, lambda z: mag.at[both, :, z], lambda z: z_one.at[both, :, z])
    zg_moves = z_moves(2, lambda z: gE.at[pl.ds(0, 3), pl.ds(1, n), z], lambda z: z_one.at[pl.ds(2, 3), :, z])
    z_one_all = [
        move(2 + i, z_one.at[:, :, pl.ds(theirs, 1)], z_one.at[:, :, pl.ds(theirs, 1)], 0, dz)
        for i, (dz, _, theirs) in enumerate(Z_WAYS)
    ]
    zw_moves = z_moves(4, lambda z: wE.at[both, :, z], lambda z: z_two.at[:, w_rows, z])
    zh_moves = z_moves(4, lambda z: hE.at[both, pl.ds(1, n), z], lambda z: z_two.at[:, h_rows, z])
    z_two_all = [
        move(4 + i, z_two.at[:, :, pl.ds(theirs, 1)], z_two.at[:, :, pl.ds(theirs, 1)], 0, dz)
        for i, (dz, _, theirs) in enumerate(Z_WAYS)
    ]

    zero = jnp.zeros((nz, nx), jnp.float32)
    for part in (0, 2):
        bE[part, 0] = zero
        bE[part, n + 1] = zero

    def wide(tile):
        return jnp.concatenate([tile] * (nx // LANES), axis=1)

    lane = lax.broadcasted_iota(jnp.int32, (nz, LANES), 1)
    sub = wide(lax.broadcasted_iota(jnp.int32, (nz, LANES), 0))
    flag = jnp.where(
        sub == nz - 1, has_high.astype(jnp.int32), jnp.where(sub == 0, has_low.astype(jnp.int32), 0)
    )
    active = flag > 0
    sign = jnp.where(sub == 0, -1.0, 1.0)

    def rim(halo):
        return jnp.where(active, sign * halo, 0.0)

    square = (
        lax.broadcasted_iota(jnp.int32, (nz, nz), 0) == lax.broadcasted_iota(jnp.int32, (nz, nz), 1)
    )
    rate_load.wait()
    r = jnp.sum(jnp.where(square, jnp.broadcast_to(rate_row[...], (nz, nz)), 0.0), axis=1, keepdims=True)
    r = jnp.broadcast_to(r, (nz, LANES))
    one = jnp.ones((nz, LANES), jnp.float32)

    r_inv = 1.0 / r
    whole, grown = one, one
    sizes = [one]
    for k in range(n):
        grown = grown + r_inv * whole
        whole = whole + grown
        sizes.append(whole)
    full_inv = 1.0 / whole
    for k in range(n):
        m = sizes[k] / sizes[k + 1]
        m_tab[k] = m
        inv_tab[k] = m * r_inv
        al_tab[n - 1 - k] = sizes[k] * full_inv
    aa, cc = sizes[n - 1] * full_inv, full_inv

    def reach(k, s):
        s_tab[k] = s
        den = cc / (1.0 - s * aa)
        den_tab[k] = den
        return aa + cc * s * den

    lax.fori_loop(0, groups, reach, jnp.zeros((nz, LANES), jnp.float32), unroll=groups <= 8)
    s_low, s_high = s_tab[me], s_tab[groups - 1 - me]
    from_low, from_high = den_tab[me] * s_low, den_tab[groups - 1 - me] * s_high
    for k in range(n):
        near, far = al_tab[k] * r_inv, al_tab[n - 1 - k] * r_inv
        w_tab[0, k] = far + from_low * near
        w_tab[1, k] = near + from_high * far

    def gather(slot):
        copies = []
        for k in range(1, groups):
            partner = lax.rem(me + k, groups)
            copies.append(pltpu.make_async_remote_copy(
                src_ref=sums.at[slot, (partner < me).astype(jnp.int32)], dst_ref=ends.at[slot, k - 1],
                send_sem=gs_sem.at[slot], recv_sem=gr_sem.at[slot],
                device_id={"gy": partner, "gz": lay}, device_id_type=MESH,
            ))
        return copies

    def gather_all(slot):
        return pltpu.make_async_remote_copy(
            src_ref=ends.at[slot], dst_ref=ends.at[slot], send_sem=gs_sem.at[slot], recv_sem=gr_sem.at[slot],
            device_id={"gy": lax.rem(me + 1, groups), "gz": lay}, device_id_type=MESH)

    nothing = (zero,) * 6

    def collect(totals, k, rows):
        toward = (wide(w_tab[0, k]), wide(w_tab[1, k]))
        return tuple(totals[3 * way + c] + toward[way] * rows[c] for way in range(2) for c in range(3))

    def put_sums(slot, totals):
        for way in range(2):
            for c in range(3):
                sums[slot, way, c] = totals[3 * way + c]

    loads[0].wait()
    totals = nothing
    for k in range(n):
        totals = collect(totals, k, [wE[c, k + 1] for c in range(3)])
    put_sums(0, totals)

    pl.semaphore_wait(barrier, count)
    start(zb_moves)
    for copy in gather(0):
        copy.start()
    start(yb_moves)
    start(yk_moves)
    start(yc_moves)

    def slope_x(f):
        tiles = [f[:, at:at + LANES] for at in range(0, nx, LANES)]
        ahead = [pltpu.roll(tile, LANES - 1, 1) for tile in tiles] + [jnp.zeros_like(tiles[0])]
        behind = [jnp.zeros_like(tiles[0])] + [pltpu.roll(tile, 1, 1) for tile in tiles]
        return jnp.concatenate(
            [
                jnp.where(lane == LANES - 1, ahead[t + 1], ahead[t])
                - jnp.where(lane == 0, behind[t], behind[t + 1])
                for t in range(len(tiles))
            ],
            axis=1,
        )

    def slope_z(f):
        ahead = jnp.where(sub == nz - 1, 0.0, pltpu.roll(f, nz - 1, 0))
        behind = jnp.where(sub == 0, 0.0, pltpu.roll(f, 1, 0))
        return ahead - behind

    def curl(field, y, extra=None, comps=(0, 1, 2)):
        f = [field[c, y + 1] for c in comps]
        dy_x = field[comps[0], y + 2] - field[comps[0], y]
        dy_z = field[comps[2], y + 2] - field[comps[2], y]
        dz_x, dz_y = slope_z(f[0]), slope_z(f[1])
        if extra is not None:
            dz_x, dz_y = dz_x + extra[0], dz_y + extra[1]
        return (dy_z - dz_y, dz_x - slope_x(f[2]), slope_x(f[1]) - dy_x), f

    def each_row(body):
        for y in range(n):
            body(y)

    loads[1].wait()
    pltpu.make_async_copy(z_one.at[pl.ds(0, 2)], z_one.at[pl.ds(2, 2)], load_sem.at[3]).wait()
    loads[4].wait()

    def argument(y):
        turn, b = curl(bE, y)
        s = [v[c, y] for c in range(3)]
        sp = gE[SPREAD, y + 1] * (0.5 - 0.5 * (1.0 - iron_factor) * iron[y].astype(jnp.float32))
        gE[1, y + 1] = s[1] * b[2] - s[2] * b[1] - sp * turn[0]
        gE[0, y + 1] = s[2] * b[0] - s[0] * b[2] - sp * turn[1]
        gE[SPREAD, y + 1] = sp
        gE[3, y + 1] = s[0] * b[1] - s[1] * b[0] - sp * turn[2]

    each_row(argument)
    start(zg_moves)
    start(yg_moves)

    def local_solve(field, offset):
        def down(k, held):
            m = wide(m_tab[jnp.maximum(k - 1, 0)])
            rows = tuple(field[c, offset + k] + m * held[c] for c in range(3))
            for c in range(3):
                field[c, offset + k] = rows[c]
            return rows

        lax.fori_loop(0, n, down, (zero, zero, zero), unroll=True)

        def up(step, held):
            k = n - 1 - step
            m, inv = wide(m_tab[k]), wide(inv_tab[k])
            rows = tuple(field[c, offset + k] * inv + m * held[c] for c in range(3))
            for c in range(3):
                field[c, offset + k] = rows[c]
            return rows

        lax.fori_loop(0, n, up, (zero, zero, zero), unroll=True)

    left_gap, right_gap = 1.0 - s_low * aa, 1.0 - s_high * aa
    det = 1.0 / (left_gap * right_gap - s_low * s_high * cc * cc)
    ll, lr = right_gap * det, s_low * cc * det
    rr, rl = left_gap * det, s_high * cc * det
    mix[0] = ll * s_low
    mix[1] = lr * s_high
    mix[2] = rl * s_low
    mix[3] = rr * s_high
    low = one
    for k in range(1, groups):
        @pl.when(k <= me)
        def _(low=low):
            coef[0, k - 1] = ll * low
            coef[1, k - 1] = rl * low

        low = low * den_tab[jnp.maximum(me - k, 0)]
    high = one
    for k in range(1, groups):
        @pl.when(k <= groups - 1 - me)
        def _(high=high):
            coef[0, groups - k - 1] = lr * high
            coef[1, groups - k - 1] = rr * high

        high = high * den_tab[jnp.maximum(groups - 1 - me - k, 0)]

    local_solve(wE, 1)

    def interface(slot, field, offset):
        first = [field[c, offset] for c in range(3)]
        last = [field[c, offset + n - 1] for c in range(3)]
        lefts, rights = [], []
        for c in range(3):
            left = wide(mix[0]) * first[c] + wide(mix[1]) * last[c]
            right = wide(mix[2]) * first[c] + wide(mix[3]) * last[c]
            for k in range(groups - 1):
                end = ends[slot, k, c]
                left = left + wide(coef[0, k]) * end
                right = right + wide(coef[1, k]) * end
            lefts.append(left)
            rights.append(right)
        return lefts, rights

    gather_all(0).wait_recv()
    lefts, rights = interface(0, wE, 1)
    for c in range(3):
        wE[c, 0] = lefts[c]
        wE[c, n + 1] = rights[c]

    def relax(y):
        near, far = wide(al_tab[y]), wide(al_tab[n - 1 - y])
        for c in range(3):
            wE[c, y + 1] = wE[c, y + 1] + near * wE[c, 0] + far * wE[c, n + 1]

    each_row(relax)
    start(zw_moves)

    def pull(y):
        turn, w = curl(wE, y)
        s = [v[c, y] for c in range(3)]
        sp = gE[SPREAD, y + 1]
        adj[0, y] = w[0] + half * (turn[1] * s[2] - turn[2] * s[1])
        adj[1, y] = w[1] + half * (turn[2] * s[0] - turn[0] * s[2])
        adj[2, y] = w[2] + half * (turn[0] * s[1] - turn[1] * s[0])
        for c in range(3):
            hE[c, y + 1] = sp * turn[c]

    each_row(pull)
    start(zh_moves)

    arrive(y_all + yk_moves + z_one_all)
    leave(y_all + z_one_all)

    for side, way in SIDES:
        have = (has_left, has_right)[side]
        edge, halo, y = (1, 0, 0) if side == 0 else (n, n + 1, n - 1)
        beyond, sp = way * y_one[side, NEAR_SPREAD], way * gE[SPREAD, edge]
        g_x = y_one[side, 4] + beyond * (bE[2, edge] + way * rim(yk[side, 0]))
        g_z = y_one[side, 6] - beyond * bE[0, edge]
        gE[1, halo] = jnp.where(have, g_x, 0.0)
        gE[3, halo] = jnp.where(have, g_z, 0.0)
        gE[1, edge] = gE[1, edge] - jnp.where(have, sp * y_one[side, 1], 0.0)
        gE[3, edge] = gE[3, edge] + jnp.where(have, sp * y_one[side, 0], 0.0)
        z_one[3, y] = z_one[3, y] - jnp.where(have, way * z_one[2 + SPREAD, y] * yk[side, 1], 0.0)

    def mend_argument(y):
        sp = gE[SPREAD, y + 1]
        gE[1, y + 1] = gE[1, y + 1] + sp * rim(z_one[1, y])
        gE[0, y + 1] = gE[0, y + 1] - sp * rim(z_one[0, y])

    each_row(mend_argument)

    totals = nothing
    for y in range(n):
        b = [bE[c, y + 1] for c in range(3)]
        sp = z_one[2 + SPREAD, y]
        extra = (
            jnp.where(active, sign * z_one[3, y] - sp * b[1], 0.0),
            jnp.where(active, sign * z_one[2, y] + sp * b[0], 0.0),
        )
        turn, _ = curl(gE, y, extra, G_COMPS)
        rows = [b[c] + half * turn[c] for c in range(3)]
        for c in range(3):
            new[c, y] = rows[c]
        totals = collect(totals, y, rows)
    put_sums(1, totals)
    for copy in gather(1):
        copy.start()

    wide_inv = wide(r_inv)
    for side, way in SIDES:
        have = (has_left, has_right)[side]
        edge, halo = (1, 0) if side == 0 else (n, n + 1)
        sp = y_one[side, NEAR_SPREAD]
        slope = {}
        for c in (0, 2):
            near, rim_row = wE[c, edge], wE[c, halo]
            outer = rim_row + (rim_row - near) + wide_inv * (rim_row - y_one[side, 2 + c // 2])
            slope[c] = way * (outer - near)
        cross = wE[1, halo]
        hE[0, halo] = jnp.where(have, sp * (slope[2] - slope_z(cross)), 0.0)
        hE[2, halo] = jnp.where(have, sp * (slope_x(cross) - slope[0]), 0.0)

    local_solve(new, 0)
    arrive(z_two_all)
    leave(z_two_all)

    for side, way in SIDES:
        have = (has_left, has_right)[side]
        halo = 0 if side == 0 else n + 1
        hE[0, halo] = hE[0, halo] - jnp.where(have, y_one[side, NEAR_SPREAD] * rim(z_two[1, halo]), 0.0)

    def mend_pull(y):
        c_x, c_y = rim(z_two[0, y + 1]), rim(z_two[1, y + 1])
        sp = gE[SPREAD, y + 1]
        s = [v[c, y] for c in range(3)]
        hE[0, y + 1] = hE[0, y + 1] - sp * c_y
        hE[1, y + 1] = hE[1, y + 1] + sp * c_x
        h_x, h_y = half * c_x, half * c_y
        adj[0, y] = adj[0, y] + h_x * s[2]
        adj[1, y] = adj[1, y] + h_y * s[2]
        adj[2, y] = adj[2, y] - (h_y * s[1] + h_x * s[0])

    each_row(mend_pull)

    def finish_adjoint(y):
        sp = z_one[2 + SPREAD, y]
        extra = (
            jnp.where(active, sign * z_two[0, n + 2 + y] + sp * wE[1, y + 1], 0.0),
            jnp.where(active, sign * z_two[1, n + 2 + y] - sp * wE[0, y + 1], 0.0),
        )
        turn, _ = curl(hE, y, extra)
        for c in range(3):
            adj[c, y] = adj[c, y] - half * turn[c]

    each_row(finish_adjoint)

    gather_all(1).wait_recv()
    lefts, rights = interface(1, new, 0)

    def finish(y):
        near, far = wide(al_tab[y]), wide(al_tab[n - 1 - y])
        for c in range(3):
            new[c, y] = new[c, y] + near * lefts[c] + far * rights[c]

    each_row(finish)

    leave(yk_moves)
    for slot in range(2):
        gather_all(slot).wait_send()


def hand_over(new, adj, new_out, adj_out, sem):
    copies = [
        pltpu.make_async_copy(new, new_out, sem.at[0]),
        pltpu.make_async_copy(adj, adj_out, sem.at[1]),
    ]
    for copy in copies:
        copy.start()
    for copy in copies:
        copy.wait()


def local(groups, layers, magnetic, velocity, diffusivity, material, plane_rate, cotangent):
    _, n, nz, nx = magnetic.shape
    block = (3, n, nz, nx)
    rimmed = (3, n + 2, nz, nx)
    f32 = jnp.float32
    anywhere = pl.BlockSpec(memory_space=pl.ANY)
    inside = pl.BlockSpec(memory_space=pltpu.VMEM)
    args = [
        pltpu.with_memory_space_constraint(array, pltpu.HBM)
        for array in (magnetic, velocity, diffusivity, material, plane_rate.reshape(1, nz), cotangent)
    ]
    new, adj = pl.pallas_call(
        functools.partial(kernel, groups, layers, n),
        out_shape=[jax.ShapeDtypeStruct(block, f32)] * 2,
        in_specs=[anywhere] * 6,
        out_specs=[inside] * 2,
        scratch_shapes=[
            pltpu.VMEM(rimmed, f32),
            pltpu.VMEM((4, n + 2, nz, nx), f32),
            pltpu.VMEM(rimmed, f32),
            pltpu.VMEM(rimmed, f32),
            pltpu.VMEM(block, f32),
            pltpu.VMEM((n, nz, nx), jnp.int32),
            pltpu.VMEM((1, nz), f32),
            pltpu.VMEM((5, n, nz, nx), f32),
            pltpu.VMEM((2, 2 * n + 2, nz, nx), f32),
            pltpu.VMEM((2, 7, nz, nx), f32),
            pltpu.VMEM((2, 2, nz, nx), f32),
            pltpu.VMEM((2, groups - 1, 3, nz, nx), f32),
            pltpu.VMEM((2, 2, 3, nz, nx), f32),
            pltpu.VMEM((n, nz, LANES), f32),
            pltpu.VMEM((n, nz, LANES), f32),
            pltpu.VMEM((n, nz, LANES), f32),
            pltpu.VMEM((groups, nz, LANES), f32),
            pltpu.VMEM((groups, nz, LANES), f32),
            pltpu.VMEM((2, n, nz, LANES), f32),
            pltpu.VMEM((4, nz, LANES), f32),
            pltpu.VMEM((2, groups - 1, nz, LANES), f32),
            pltpu.SemaphoreType.DMA((5,)),
            pltpu.SemaphoreType.DMA((N_WAYS,)),
            pltpu.SemaphoreType.DMA((N_WAYS,)),
            pltpu.SemaphoreType.DMA((2,)),
            pltpu.SemaphoreType.DMA((2,)),
        ],
        compiler_params=pltpu.CompilerParams(
            collective_id=0, has_side_effects=True, vmem_limit_bytes=24 * 2**20
        ),
    )(*args)
    return tuple(pl.pallas_call(
        hand_over,
        out_shape=[jax.ShapeDtypeStruct(block, f32)] * 2,
        in_specs=[anywhere] * 2,
        out_specs=[anywhere] * 2,
        scratch_shapes=[pltpu.SemaphoreType.DMA((2,))],
        compiler_params=pltpu.CompilerParams(vmem_limit_bytes=2**20),
    )(new, adj))


def solution(mesh):
    in_specs = (
        P(None, "gy", "gz", None),
        P(None, "gy", "gz", None),
        P("gy", "gz", None),
        P("gy", "gz", None),
        P("gz"),
        P(None, "gy", "gz", None),
    )
    out_specs = (P(None, "gy", "gz", None), P(None, "gy", "gz", None))
    body = functools.partial(local, mesh.shape["gy"], mesh.shape["gz"])
    return jax.shard_map(body, mesh=mesh, in_specs=in_specs, out_specs=out_specs, check_vma=False)
```

```python
import functools
import jax
import jax.numpy as jnp
from jax import lax
from jax.experimental import pallas as pl
from jax.experimental.pallas import tpu as pltpu
from jax.sharding import PartitionSpec as P

step_size = 0.1
iron_factor = 0.2
MESH = pl.DeviceIdType.MESH
LANES = 128
SIDES = ((0, -1), (1, 1))
N_WAYS = 10
G_COMPS = (1, 0, 3)
SPREAD = 2
NEAR_SPREAD = 5


def kernel(
    groups, layers, n, mag, vel, dif, mat, rate, cot, new, adj,
    bE, gE, wE, hE, tE, v, iron, rate_row, z_one, z_two, y_one, yk, ends, sums,
    m_tab, inv_tab, al_tab, s_tab, den_tab, w_tab, mix, coef, chain,
    load_sem, send_sem, recv_sem, gs_sem, gr_sem,
):
    me = lax.axis_index("gy")
    lay = lax.axis_index("gz")
    nx = bE.shape[-1]
    nz = bE.shape[-2]
    half = 0.5 * step_size

    rate_load = pltpu.make_async_copy(rate, rate_row, load_sem.at[4])
    rate_load.start()
    loads = [
        pltpu.make_async_copy(cot, wE.at[:, pl.ds(1, n)], load_sem.at[1]),
        pltpu.make_async_copy(mag, bE.at[:, pl.ds(1, n)], load_sem.at[0]),
        pltpu.make_async_copy(dif, gE.at[SPREAD, pl.ds(1, n)], load_sem.at[3]),
        pltpu.make_async_copy(mat, iron, load_sem.at[3]),
        pltpu.make_async_copy(vel, v, load_sem.at[2]),
    ]
    for load in loads:
        load.start()

    has_left, has_right = me > 0, me < groups - 1
    has_low, has_high = lay > 0, lay < layers - 1

    def there(dy, dz):
        found = None
        for step, low, high in ((dy, has_left, has_right), (dz, has_low, has_high)):
            if step:
                seen = low if step < 0 else high
                found = seen if found is None else jnp.logical_and(found, seen)
        return found

    def place(dy, dz):
        return {
            "gy": jnp.clip(me + dy, 0, groups - 1) if dy else me,
            "gz": jnp.clip(lay + dz, 0, layers - 1) if dz else lay,
        }

    around = [(dy, dz) for dy in (-1, 0, 1) for dz in (-1, 0, 1) if dz]
    barrier = pltpu.get_barrier_semaphore()
    for k in range(1, groups):
        pl.semaphore_signal(
            barrier, inc=1, device_id={"gy": lax.rem(me + k, groups), "gz": lay}, device_id_type=MESH
        )
    count = jnp.int32(groups - 1)
    for dy, dz in around:
        count = count + there(dy, dz).astype(jnp.int32)

        @pl.when(there(dy, dz))
        def _():
            pl.semaphore_signal(barrier, inc=1, device_id=place(dy, dz), device_id_type=MESH)

    def move(slot, src, dst, dy, dz):
        copy = pltpu.make_async_remote_copy(
            src_ref=src, dst_ref=dst, send_sem=send_sem.at[slot], recv_sem=recv_sem.at[slot],
            device_id=place(dy, dz), device_id_type=MESH)
        return copy, there(dy, dz), there(-dy, -dz)

    def start(moves):
        for copy, ahead, _ in moves:
            @pl.when(ahead)
            def _():
                copy.start()

    def arrive(moves):
        for copy, _, behind in moves:
            @pl.when(behind)
            def _():
                copy.wait_recv()

    def leave(moves):
        for copy, ahead, _ in moves:
            @pl.when(ahead)
            def _():
                copy.wait_send()

    Y_WAYS = ((-1, 0, 1), (1, n - 1, 0))
    Z_WAYS = ((-1, 0, nz - 1), (1, nz - 1, 0))

    def y_moves(slot, src, dst, first):
        return [
            move(slot + i, src(first + row), dst(side), dy, 0)
            for i, (dy, row, side) in enumerate(Y_WAYS)
        ]

    def z_moves(slot, src, dst):
        return [
            move(slot + i, src(pl.ds(mine, 1)), dst(pl.ds(theirs, 1)), 0, dz)
            for i, (dz, mine, theirs) in enumerate(Z_WAYS)
        ]

    yb_moves = [
        copy for i, c in enumerate((0, 2))
        for copy in y_moves(0, lambda row: mag.at[c, row], lambda side: y_one.at[side, i], 0)
    ]
    yc_moves = [
        copy for i, c in enumerate((0, 2))
        for copy in y_moves(0, lambda row: cot.at[c, row], lambda side: y_one.at[side, 2 + i], 0)
    ]
    yg_moves = y_moves(0, lambda row: gE.at[pl.ds(1, 3), row], lambda side: y_one.at[side, pl.ds(4, 3)], 1)
    y_all = [
        move(i, y_one.at[side], y_one.at[side], dy, 0) for i, (dy, _, side) in enumerate(Y_WAYS)
    ]
    yk_moves = [
        move(
            6 + 2 * i + j, mag.at[pl.ds(1, 2), row, pl.ds(mine, 1)], yk.at[side, :, pl.ds(theirs, 1)], dy, dz
        )
        for i, (dy, row, side) in enumerate(Y_WAYS)
        for j, (dz, mine, theirs) in enumerate(Z_WAYS)
    ]
    both = pl.ds(0, 2)
    w_rows, h_rows = pl.ds(0, n + 2), pl.ds(n + 2, n)
    zb_moves = z_moves(2, lambda z: mag.at[both, :, z], lambda z: z_one.at[both, :, z])
    zg_moves = z_moves(2, lambda z: gE.at[pl.ds(0, 3), pl.ds(1, n), z], lambda z: z_one.at[pl.ds(2, 3), :, z])
    z_one_all = [
        move(2 + i, z_one.at[:, :, pl.ds(theirs, 1)], z_one.at[:, :, pl.ds(theirs, 1)], 0, dz)
        for i, (dz, _, theirs) in enumerate(Z_WAYS)
    ]
    zw_moves = z_moves(4, lambda z: wE.at[both, :, z], lambda z: z_two.at[:, w_rows, z])
    zh_moves = z_moves(4, lambda z: hE.at[both, pl.ds(1, n), z], lambda z: z_two.at[:, h_rows, z])
    z_two_all = [
        move(4 + i, z_two.at[:, :, pl.ds(theirs, 1)], z_two.at[:, :, pl.ds(theirs, 1)], 0, dz)
        for i, (dz, _, theirs) in enumerate(Z_WAYS)
    ]

    zero = jnp.zeros((nz, nx), jnp.float32)
    for part in (0, 2):
        bE[part, 0] = zero
        bE[part, n + 1] = zero

    def wide(tile):
        return jnp.concatenate([tile] * (nx // LANES), axis=1)

    lane = lax.broadcasted_iota(jnp.int32, (nz, LANES), 1)
    sub = wide(lax.broadcasted_iota(jnp.int32, (nz, LANES), 0))
    flag = jnp.where(
        sub == nz - 1, has_high.astype(jnp.int32), jnp.where(sub == 0, has_low.astype(jnp.int32), 0)
    )
    active = flag > 0
    sign = jnp.where(sub == 0, -1.0, 1.0)

    def rim(halo):
        return jnp.where(active, sign * halo, 0.0)

    square = (
        lax.broadcasted_iota(jnp.int32, (nz, nz), 0) == lax.broadcasted_iota(jnp.int32, (nz, nz), 1)
    )
    rate_load.wait()
    r = jnp.sum(jnp.where(square, jnp.broadcast_to(rate_row[...], (nz, nz)), 0.0), axis=1, keepdims=True)
    r = jnp.broadcast_to(r, (nz, LANES))
    one = jnp.ones((nz, LANES), jnp.float32)

    r_inv = 1.0 / r
    whole, grown = one, one
    sizes = [one]
    for k in range(n):
        grown = grown + r_inv * whole
        whole = whole + grown
        sizes.append(whole)
    full_inv = 1.0 / whole
    for k in range(n):
        m = sizes[k] / sizes[k + 1]
        m_tab[k] = m
        inv_tab[k] = m * r_inv
        al_tab[n - 1 - k] = sizes[k] * full_inv
    aa, cc = sizes[n - 1] * full_inv, full_inv

    def reach(k, s):
        s_tab[k] = s
        den = cc / (1.0 - s * aa)
        den_tab[k] = den
        return aa + cc * s * den

    lax.fori_loop(0, groups, reach, jnp.zeros((nz, LANES), jnp.float32), unroll=groups <= 8)
    s_low, s_high = s_tab[me], s_tab[groups - 1 - me]
    from_low, from_high = den_tab[me] * s_low, den_tab[groups - 1 - me] * s_high
    for k in range(n):
        near, far = al_tab[k] * r_inv, al_tab[n - 1 - k] * r_inv
        w_tab[0, k] = far + from_low * near
        w_tab[1, k] = near + from_high * far

    def gather(slot):
        copies = []
        for k in range(groups - 1):
            above = (me <= k).astype(jnp.int32)
            partner = k + above
            copies.append(pltpu.make_async_remote_copy(
                src_ref=sums.at[slot, 1 - above], dst_ref=ends.at[slot, me - 1 + above],
                send_sem=gs_sem.at[slot], recv_sem=gr_sem.at[slot],
                device_id={"gy": partner, "gz": lay}, device_id_type=MESH,
            ))
        return copies

    def gather_all(slot):
        return pltpu.make_async_remote_copy(
            src_ref=ends.at[slot], dst_ref=ends.at[slot], send_sem=gs_sem.at[slot], recv_sem=gr_sem.at[slot],
            device_id={"gy": lax.rem(me + 1, groups), "gz": lay}, device_id_type=MESH)

    nothing = (zero,) * 6

    def collect(totals, k, rows):
        toward = (wide(w_tab[0, k]), wide(w_tab[1, k]))
        return tuple(totals[3 * way + c] + toward[way] * rows[c] for way in range(2) for c in range(3))

    def put_sums(slot, totals):
        for way in range(2):
            for c in range(3):
                sums[slot, way, c] = totals[3 * way + c]

    loads[0].wait()
    totals = nothing
    for k in range(n):
        totals = collect(totals, k, [wE[c, k + 1] for c in range(3)])
    put_sums(0, totals)

    pl.semaphore_wait(barrier, count)
    start(yk_moves)
    for copy in gather(0):
        copy.start()
    start(zb_moves)
    start(yb_moves)

    def slope_x(f):
        tiles = [f[:, at:at + LANES] for at in range(0, nx, LANES)]
        ahead = [pltpu.roll(tile, LANES - 1, 1) for tile in tiles] + [jnp.zeros_like(tiles[0])]
        behind = [jnp.zeros_like(tiles[0])] + [pltpu.roll(tile, 1, 1) for tile in tiles]
        return jnp.concatenate(
            [
                jnp.where(lane == LANES - 1, ahead[t + 1], ahead[t])
                - jnp.where(lane == 0, behind[t], behind[t + 1])
                for t in range(len(tiles))
            ],
            axis=1,
        )

    def slope_z(f):
        ahead = jnp.where(sub == nz - 1, 0.0, pltpu.roll(f, nz - 1, 0))
        behind = jnp.where(sub == 0, 0.0, pltpu.roll(f, 1, 0))
        return ahead - behind

    def curl(field, y, extra=None, comps=(0, 1, 2)):
        f = [field[c, y + 1] for c in comps]
        dy_x = field[comps[0], y + 2] - field[comps[0], y]
        dy_z = field[comps[2], y + 2] - field[comps[2], y]
        dz_x, dz_y = slope_z(f[0]), slope_z(f[1])
        if extra is not None:
            dz_x, dz_y = dz_x + extra[0], dz_y + extra[1]
        return (dy_z - dz_y, dz_x - slope_x(f[2]), slope_x(f[1]) - dy_x), f

    def each_row(body):
        for y in range(n):
            body(y)

    loads[1].wait()
    pltpu.make_async_copy(z_one.at[pl.ds(0, 2)], z_one.at[pl.ds(2, 2)], load_sem.at[3]).wait()
    loads[4].wait()

    def argument(y):
        turn, b = curl(bE, y)
        s = [v[c, y] for c in range(3)]
        sp = gE[SPREAD, y + 1] * (0.5 - 0.5 * (1.0 - iron_factor) * iron[y].astype(jnp.float32))
        gE[1, y + 1] = s[1] * b[2] - s[2] * b[1] - sp * turn[0]
        gE[0, y + 1] = s[2] * b[0] - s[0] * b[2] - sp * turn[1]
        gE[SPREAD, y + 1] = sp
        gE[3, y + 1] = s[0] * b[1] - s[1] * b[0] - sp * turn[2]

    each_row(argument)
    start(zg_moves)
    start(yg_moves)
    start(yc_moves)

    def local_solve(field, offset):
        def down(k, held):
            m = wide(m_tab[jnp.maximum(k - 1, 0)])
            rows = tuple(field[c, offset + k] + m * held[c] for c in range(3))
            for c in range(3):
                field[c, offset + k] = rows[c]
            return rows

        lax.fori_loop(0, n, down, (zero, zero, zero), unroll=True)

        def up(step, held):
            k = n - 1 - step
            m, inv = wide(m_tab[k]), wide(inv_tab[k])
            rows = tuple(field[c, offset + k] * inv + m * held[c] for c in range(3))
            for c in range(3):
                field[c, offset + k] = rows[c]
            return rows

        lax.fori_loop(0, n, up, (zero, zero, zero), unroll=True)

    left_gap, right_gap = 1.0 - s_low * aa, 1.0 - s_high * aa
    det = 1.0 / (left_gap * right_gap - s_low * s_high * cc * cc)
    ll, lr = right_gap * det, s_low * cc * det
    rr, rl = left_gap * det, s_high * cc * det
    mix[0] = ll * s_low
    mix[1] = lr * s_high
    mix[2] = rl * s_low
    mix[3] = rr * s_high
    low, high = one, one
    for k in range(1, groups):
        chain[0, k] = low
        chain[1, k] = high
        low = low * den_tab[jnp.maximum(me - k, 0)]
        high = high * den_tab[jnp.maximum(groups - 1 - me - k, 0)]
    for k in range(groups - 1):
        below = k < me
        reached = chain[jnp.where(below, 0, 1), jnp.where(below, me - k, k + 1 - me)]
        coef[0, k] = reached * jnp.where(below, ll, lr)
        coef[1, k] = reached * jnp.where(below, rl, rr)

    local_solve(wE, 1)

    def interface(slot, field, offset):
        first = [field[c, offset] for c in range(3)]
        last = [field[c, offset + n - 1] for c in range(3)]
        lefts, rights = [], []
        for c in range(3):
            left = wide(mix[0]) * first[c] + wide(mix[1]) * last[c]
            right = wide(mix[2]) * first[c] + wide(mix[3]) * last[c]
            for k in range(groups - 1):
                end = ends[slot, k, c]
                left = left + wide(coef[0, k]) * end
                right = right + wide(coef[1, k]) * end
            lefts.append(left)
            rights.append(right)
        return lefts, rights

    gather_all(0).wait_recv()
    lefts, rights = interface(0, wE, 1)
    for c in range(3):
        wE[c, 0] = lefts[c]
        wE[c, n + 1] = rights[c]

    def relax(y):
        near, far = wide(al_tab[y]), wide(al_tab[n - 1 - y])
        for c in range(3):
            wE[c, y + 1] = wE[c, y + 1] + near * wE[c, 0] + far * wE[c, n + 1]

    each_row(relax)
    start(zw_moves)

    def pull(y):
        turn, _ = curl(wE, y)
        sp = gE[SPREAD, y + 1]
        for c in range(3):
            tE[c, y] = turn[c]
            hE[c, y + 1] = sp * turn[c]

    each_row(pull)
    start(zh_moves)

    arrive(y_all + yk_moves + z_one_all)
    leave(y_all + z_one_all)

    for side, way in SIDES:
        have = (has_left, has_right)[side]
        edge, halo, y = (1, 0, 0) if side == 0 else (n, n + 1, n - 1)
        beyond, sp = way * y_one[side, NEAR_SPREAD], way * gE[SPREAD, edge]
        g_x = y_one[side, 4] + beyond * (bE[2, edge] + way * rim(yk[side, 0]))
        g_z = y_one[side, 6] - beyond * bE[0, edge]
        gE[1, halo] = jnp.where(have, g_x, 0.0)
        gE[3, halo] = jnp.where(have, g_z, 0.0)
        gE[1, edge] = gE[1, edge] - jnp.where(have, sp * y_one[side, 1], 0.0)
        gE[3, edge] = gE[3, edge] + jnp.where(have, sp * y_one[side, 0], 0.0)
        z_one[3, y] = z_one[3, y] - jnp.where(have, way * z_one[2 + SPREAD, y] * yk[side, 1], 0.0)

    def mend_argument(y):
        sp = gE[SPREAD, y + 1]
        gE[1, y + 1] = gE[1, y + 1] + sp * rim(z_one[1, y])
        gE[0, y + 1] = gE[0, y + 1] - sp * rim(z_one[0, y])

    each_row(mend_argument)

    totals = nothing
    for y in range(n):
        b = [bE[c, y + 1] for c in range(3)]
        sp = z_one[2 + SPREAD, y]
        extra = (
            jnp.where(active, sign * z_one[3, y] - sp * b[1], 0.0),
            jnp.where(active, sign * z_one[2, y] + sp * b[0], 0.0),
        )
        turn, _ = curl(gE, y, extra, G_COMPS)
        rows = [b[c] + half * turn[c] for c in range(3)]
        for c in range(3):
            new[c, y] = rows[c]
        totals = collect(totals, y, rows)
    put_sums(1, totals)
    for copy in gather(1):
        copy.start()

    def pull_field(y):
        turn = [tE[c, y] for c in range(3)]
        s = [v[c, y] for c in range(3)]
        adj[0, y] = wE[0, y + 1] + half * (turn[1] * s[2] - turn[2] * s[1])
        adj[1, y] = wE[1, y + 1] + half * (turn[2] * s[0] - turn[0] * s[2])
        adj[2, y] = wE[2, y + 1] + half * (turn[0] * s[1] - turn[1] * s[0])

    each_row(pull_field)
    wide_inv = wide(r_inv)
    for side, way in SIDES:
        have = (has_left, has_right)[side]
        edge, halo = (1, 0) if side == 0 else (n, n + 1)
        sp = y_one[side, NEAR_SPREAD]
        slope = {}
        for c in (0, 2):
            near, rim_row = wE[c, edge], wE[c, halo]
            outer = rim_row + (rim_row - near) + wide_inv * (rim_row - y_one[side, 2 + c // 2])
            slope[c] = way * (outer - near)
        cross = wE[1, halo]
        hE[0, halo] = jnp.where(have, sp * (slope[2] - slope_z(cross)), 0.0)
        hE[2, halo] = jnp.where(have, sp * (slope_x(cross) - slope[0]), 0.0)

    local_solve(new, 0)
    arrive(z_two_all)
    leave(z_two_all)

    for side, way in SIDES:
        have = (has_left, has_right)[side]
        halo = 0 if side == 0 else n + 1
        hE[0, halo] = hE[0, halo] - jnp.where(have, y_one[side, NEAR_SPREAD] * rim(z_two[1, halo]), 0.0)

    def mend_pull(y):
        c_x, c_y = rim(z_two[0, y + 1]), rim(z_two[1, y + 1])
        sp = gE[SPREAD, y + 1]
        s = [v[c, y] for c in range(3)]
        hE[0, y + 1] = hE[0, y + 1] - sp * c_y
        hE[1, y + 1] = hE[1, y + 1] + sp * c_x
        h_x, h_y = half * c_x, half * c_y
        adj[0, y] = adj[0, y] + h_x * s[2]
        adj[1, y] = adj[1, y] + h_y * s[2]
        adj[2, y] = adj[2, y] - (h_y * s[1] + h_x * s[0])

    each_row(mend_pull)

    def finish_adjoint(y):
        sp = z_one[2 + SPREAD, y]
        extra = (
            jnp.where(active, sign * z_two[0, n + 2 + y] + sp * wE[1, y + 1], 0.0),
            jnp.where(active, sign * z_two[1, n + 2 + y] - sp * wE[0, y + 1], 0.0),
        )
        turn, _ = curl(hE, y, extra)
        for c in range(3):
            adj[c, y] = adj[c, y] - half * turn[c]

    each_row(finish_adjoint)

    gather_all(1).wait_recv()
    lefts, rights = interface(1, new, 0)

    def finish(y):
        near, far = wide(al_tab[y]), wide(al_tab[n - 1 - y])
        for c in range(3):
            new[c, y] = new[c, y] + near * lefts[c] + far * rights[c]

    each_row(finish)

    leave(yk_moves)
    for slot in range(2):
        gather_all(slot).wait_send()


def hand_over(new, adj, new_out, adj_out, sem):
    copies = [
        pltpu.make_async_copy(new, new_out, sem.at[0]),
        pltpu.make_async_copy(adj, adj_out, sem.at[1]),
    ]
    for copy in copies:
        copy.start()
    for copy in copies:
        copy.wait()


def local(groups, layers, magnetic, velocity, diffusivity, material, plane_rate, cotangent):
    _, n, nz, nx = magnetic.shape
    block = (3, n, nz, nx)
    rimmed = (3, n + 2, nz, nx)
    f32 = jnp.float32
    anywhere = pl.BlockSpec(memory_space=pl.ANY)
    inside = pl.BlockSpec(memory_space=pltpu.VMEM)
    args = [
        pltpu.with_memory_space_constraint(array, pltpu.HBM)
        for array in (magnetic, velocity, diffusivity, material, plane_rate.reshape(1, nz), cotangent)
    ]
    new, adj = pl.pallas_call(
        functools.partial(kernel, groups, layers, n),
        out_shape=[jax.ShapeDtypeStruct(block, f32)] * 2,
        in_specs=[anywhere] * 6,
        out_specs=[inside] * 2,
        scratch_shapes=[
            pltpu.VMEM(rimmed, f32),
            pltpu.VMEM((4, n + 2, nz, nx), f32),
            pltpu.VMEM(rimmed, f32),
            pltpu.VMEM(rimmed, f32),
            pltpu.VMEM(block, f32),
            pltpu.VMEM(block, f32),
            pltpu.VMEM((n, nz, nx), jnp.int32),
            pltpu.VMEM((1, nz), f32),
            pltpu.VMEM((5, n, nz, nx), f32),
            pltpu.VMEM((2, 2 * n + 2, nz, nx), f32),
            pltpu.VMEM((2, 7, nz, nx), f32),
            pltpu.VMEM((2, 2, nz, nx), f32),
            pltpu.VMEM((2, groups - 1, 3, nz, nx), f32),
            pltpu.VMEM((2, 2, 3, nz, nx), f32),
            pltpu.VMEM((n, nz, LANES), f32),
            pltpu.VMEM((n, nz, LANES), f32),
            pltpu.VMEM((n, nz, LANES), f32),
            pltpu.VMEM((groups, nz, LANES), f32),
            pltpu.VMEM((groups, nz, LANES), f32),
            pltpu.VMEM((2, n, nz, LANES), f32),
            pltpu.VMEM((4, nz, LANES), f32),
            pltpu.VMEM((2, groups - 1, nz, LANES), f32),
            pltpu.VMEM((2, groups, nz, LANES), f32),
            pltpu.SemaphoreType.DMA((5,)),
            pltpu.SemaphoreType.DMA((N_WAYS,)),
            pltpu.SemaphoreType.DMA((N_WAYS,)),
            pltpu.SemaphoreType.DMA((2,)),
            pltpu.SemaphoreType.DMA((2,)),
        ],
        compiler_params=pltpu.CompilerParams(
            collective_id=0, has_side_effects=True, vmem_limit_bytes=24 * 2**20
        ),
    )(*args)
    return tuple(pl.pallas_call(
        hand_over,
        out_shape=[jax.ShapeDtypeStruct(block, f32)] * 2,
        in_specs=[anywhere] * 2,
        out_specs=[anywhere] * 2,
        scratch_shapes=[pltpu.SemaphoreType.DMA((2,))],
        compiler_params=pltpu.CompilerParams(vmem_limit_bytes=2**20),
    )(new, adj))


def solution(mesh):
    in_specs = (
        P(None, "gy", "gz", None),
        P(None, "gy", "gz", None),
        P("gy", "gz", None),
        P("gy", "gz", None),
        P("gz"),
        P(None, "gy", "gz", None),
    )
    out_specs = (P(None, "gy", "gz", None), P(None, "gy", "gz", None))
    body = functools.partial(local, mesh.shape["gy"], mesh.shape["gz"])
    return jax.shard_map(body, mesh=mesh, in_specs=in_specs, out_specs=out_specs, check_vma=False)
```

```python
import functools
import jax
import jax.numpy as jnp
from jax import lax
from jax.experimental import pallas as pl
from jax.experimental.pallas import tpu as pltpu
from jax.sharding import PartitionSpec as P

step_size = 0.1
iron_factor = 0.2
MESH = pl.DeviceIdType.MESH
LANES = 128
SIDES = ((0, -1), (1, 1))
N_WAYS = 6
G_COMPS = (1, 0, 3)
SPREAD = 2
NEAR_SPREAD = 5


def kernel(
    groups, layers, n, mag, vel, dif, mat, rate, cot, new, adj,
    bE, gE, wE, hE, tE, v, iron, rate_row, z_one, z_two, y_one, yk, ends, sums,
    m_tab, inv_tab, al_tab, s_tab, den_tab, w_tab, mix, coef, chain,
    load_sem, send_sem, recv_sem, gs_sem, gr_sem,
):
    me = lax.axis_index("gy")
    lay = lax.axis_index("gz")
    nx = bE.shape[-1]
    nz = bE.shape[-2]
    half = 0.5 * step_size

    rate_load = pltpu.make_async_copy(rate, rate_row, load_sem.at[4])
    rate_load.start()
    loads = [
        pltpu.make_async_copy(cot, wE.at[:, pl.ds(1, n)], load_sem.at[1]),
        pltpu.make_async_copy(mag, bE.at[:, pl.ds(1, n)], load_sem.at[0]),
        pltpu.make_async_copy(dif, gE.at[SPREAD, pl.ds(1, n)], load_sem.at[3]),
        pltpu.make_async_copy(mat, iron, load_sem.at[3]),
        pltpu.make_async_copy(vel, v, load_sem.at[2]),
    ]
    for load in loads:
        load.start()

    has_left, has_right = me > 0, me < groups - 1
    has_low, has_high = lay > 0, lay < layers - 1

    def there(dy, dz):
        found = None
        for step, low, high in ((dy, has_left, has_right), (dz, has_low, has_high)):
            if step:
                seen = low if step < 0 else high
                found = seen if found is None else jnp.logical_and(found, seen)
        return found

    def place(dy, dz):
        return {
            "gy": jnp.clip(me + dy, 0, groups - 1) if dy else me,
            "gz": jnp.clip(lay + dz, 0, layers - 1) if dz else lay,
        }

    around = [(dy, dz) for dy in (-1, 0, 1) for dz in (-1, 0, 1) if dz]
    barrier = pltpu.get_barrier_semaphore()
    for k in range(1, groups):
        pl.semaphore_signal(
            barrier, inc=1, device_id={"gy": lax.rem(me + k, groups), "gz": lay}, device_id_type=MESH
        )
    count = jnp.int32(groups - 1)
    for dy, dz in around:
        count = count + there(dy, dz).astype(jnp.int32)

        @pl.when(there(dy, dz))
        def _():
            pl.semaphore_signal(barrier, inc=1, device_id=place(dy, dz), device_id_type=MESH)

    def move(slot, src, dst, dy, dz):
        copy = pltpu.make_async_remote_copy(
            src_ref=src, dst_ref=dst, send_sem=send_sem.at[slot], recv_sem=recv_sem.at[slot],
            device_id=place(dy, dz), device_id_type=MESH)
        return copy, there(dy, dz), there(-dy, -dz)

    def start(moves):
        for copy, ahead, _ in moves:
            @pl.when(ahead)
            def _():
                copy.start()

    def arrive(moves):
        for copy, _, behind in moves:
            @pl.when(behind)
            def _():
                copy.wait_recv()

    def leave(moves):
        for copy, ahead, _ in moves:
            @pl.when(ahead)
            def _():
                copy.wait_send()

    Y_WAYS = ((-1, 0, 1), (1, n - 1, 0))
    Z_WAYS = ((-1, 0, nz - 1), (1, nz - 1, 0))

    def y_moves(slot, src, dst, first):
        return [
            move(slot + i, src(first + row), dst(side), dy, 0)
            for i, (dy, row, side) in enumerate(Y_WAYS)
        ]

    def z_moves(slot, src, dst):
        return [
            move(slot + i, src(pl.ds(mine, 1)), dst(pl.ds(theirs, 1)), 0, dz)
            for i, (dz, mine, theirs) in enumerate(Z_WAYS)
        ]

    yb_moves = [
        copy for i, c in enumerate((0, 2))
        for copy in y_moves(0, lambda row: mag.at[c, row], lambda side: y_one.at[side, i], 0)
    ]
    yc_moves = [
        copy for i, c in enumerate((0, 2))
        for copy in y_moves(0, lambda row: cot.at[c, row], lambda side: y_one.at[side, 2 + i], 0)
    ]
    yg_moves = y_moves(0, lambda row: gE.at[pl.ds(1, 3), row], lambda side: y_one.at[side, pl.ds(4, 3)], 1)
    yk_moves = [
        move(
            i, mag.at[pl.ds(1, 2), row, pl.ds(mine, 1)], yk.at[side, :, pl.ds(theirs, 1)], dy, dz
        )
        for i, (dy, row, side) in enumerate(Y_WAYS)
        for j, (dz, mine, theirs) in enumerate(Z_WAYS)
    ]
    both = pl.ds(0, 2)
    w_rows, h_rows = pl.ds(0, n + 2), pl.ds(n + 2, n)
    zb_moves = z_moves(2, lambda z: mag.at[both, :, z], lambda z: z_one.at[both, :, z])
    zg_moves = z_moves(2, lambda z: gE.at[pl.ds(0, 3), pl.ds(1, n), z], lambda z: z_one.at[pl.ds(2, 3), :, z])
    z_one_all = [
        move(2 + i, z_one.at[:, :, pl.ds(theirs, 1)], z_one.at[:, :, pl.ds(theirs, 1)], 0, dz)
        for i, (dz, _, theirs) in enumerate(Z_WAYS)
    ]
    layers_by = has_low.astype(jnp.int32) + has_high.astype(jnp.int32)
    y_all = []
    for i, (dy, _, _) in enumerate(Y_WAYS):
        for by in range(3):
            rows = z_two.at[:, pl.ds(0, 7 * nz // 2 + by), pl.ds(0, 1)]
            copy, ahead, behind = move(i, rows, rows, dy, 0)
            fits = layers_by == by
            y_all.append((copy, jnp.logical_and(ahead, fits), jnp.logical_and(behind, fits)))
    zw_moves = z_moves(4, lambda z: wE.at[both, :, z], lambda z: z_two.at[:, w_rows, z])
    zh_moves = z_moves(4, lambda z: hE.at[both, pl.ds(1, n), z], lambda z: z_two.at[:, h_rows, z])
    z_two_all = [
        move(4 + i, z_two.at[:, :, pl.ds(theirs, 1)], z_two.at[:, :, pl.ds(theirs, 1)], 0, dz)
        for i, (dz, _, theirs) in enumerate(Z_WAYS)
    ]

    zero = jnp.zeros((nz, nx), jnp.float32)
    for part in (0, 2):
        bE[part, 0] = zero
        bE[part, n + 1] = zero

    def wide(tile):
        return jnp.concatenate([tile] * (nx // LANES), axis=1)

    lane = lax.broadcasted_iota(jnp.int32, (nz, LANES), 1)
    sub = wide(lax.broadcasted_iota(jnp.int32, (nz, LANES), 0))
    flag = jnp.where(
        sub == nz - 1, has_high.astype(jnp.int32), jnp.where(sub == 0, has_low.astype(jnp.int32), 0)
    )
    active = flag > 0
    sign = jnp.where(sub == 0, -1.0, 1.0)

    def rim(halo):
        return jnp.where(active, sign * halo, 0.0)

    square = (
        lax.broadcasted_iota(jnp.int32, (nz, nz), 0) == lax.broadcasted_iota(jnp.int32, (nz, nz), 1)
    )
    rate_load.wait()
    r = jnp.sum(jnp.where(square, jnp.broadcast_to(rate_row[...], (nz, nz)), 0.0), axis=1, keepdims=True)
    r = jnp.broadcast_to(r, (nz, LANES))
    one = jnp.ones((nz, LANES), jnp.float32)

    r_inv = 1.0 / r
    whole, grown = one, one
    sizes = [one]
    for k in range(n):
        grown = grown + r_inv * whole
        whole = whole + grown
        sizes.append(whole)
    full_inv = 1.0 / whole
    for k in range(n):
        m = sizes[k] / sizes[k + 1]
        m_tab[k] = m
        inv_tab[k] = m * r_inv
        al_tab[n - 1 - k] = sizes[k] * full_inv
    aa, cc = sizes[n - 1] * full_inv, full_inv

    def reach(k, s):
        s_tab[k] = s
        den = cc / (1.0 - s * aa)
        den_tab[k] = den
        return aa + cc * s * den

    lax.fori_loop(0, groups, reach, jnp.zeros((nz, LANES), jnp.float32), unroll=groups <= 8)
    s_low, s_high = s_tab[me], s_tab[groups - 1 - me]
    from_low, from_high = den_tab[me] * s_low, den_tab[groups - 1 - me] * s_high
    for k in range(n):
        near, far = al_tab[k] * r_inv, al_tab[n - 1 - k] * r_inv
        w_tab[0, k] = far + from_low * near
        w_tab[1, k] = near + from_high * far

    def gather(slot):
        copies = []
        for k in range(groups - 1):
            above = (me <= k).astype(jnp.int32)
            partner = k + above
            copies.append(pltpu.make_async_remote_copy(
                src_ref=sums.at[slot, 1 - above], dst_ref=ends.at[slot, me - 1 + above],
                send_sem=gs_sem.at[slot], recv_sem=gr_sem.at[slot],
                device_id={"gy": partner, "gz": lay}, device_id_type=MESH,
            ))
        return copies

    def gather_all(slot):
        return pltpu.make_async_remote_copy(
            src_ref=ends.at[slot], dst_ref=ends.at[slot], send_sem=gs_sem.at[slot], recv_sem=gr_sem.at[slot],
            device_id={"gy": lax.rem(me + 1, groups), "gz": lay}, device_id_type=MESH)

    nothing = (zero,) * 6

    def collect(totals, k, rows):
        toward = (wide(w_tab[0, k]), wide(w_tab[1, k]))
        return tuple(totals[3 * way + c] + toward[way] * rows[c] for way in range(2) for c in range(3))

    def put_sums(slot, totals):
        for way in range(2):
            for c in range(3):
                sums[slot, way, c] = totals[3 * way + c]

    loads[0].wait()
    totals = nothing
    for k in range(n):
        totals = collect(totals, k, [wE[c, k + 1] for c in range(3)])
    put_sums(0, totals)

    pl.semaphore_wait(barrier, count)
    start(yk_moves)
    for copy in gather(0):
        copy.start()
    start(zb_moves)
    start(yb_moves)

    def slope_x(f):
        tiles = [f[:, at:at + LANES] for at in range(0, nx, LANES)]
        ahead = [pltpu.roll(tile, LANES - 1, 1) for tile in tiles] + [jnp.zeros_like(tiles[0])]
        behind = [jnp.zeros_like(tiles[0])] + [pltpu.roll(tile, 1, 1) for tile in tiles]
        return jnp.concatenate(
            [
                jnp.where(lane == LANES - 1, ahead[t + 1], ahead[t])
                - jnp.where(lane == 0, behind[t], behind[t + 1])
                for t in range(len(tiles))
            ],
            axis=1,
        )

    def slope_z(f):
        ahead = jnp.where(sub == nz - 1, 0.0, pltpu.roll(f, nz - 1, 0))
        behind = jnp.where(sub == 0, 0.0, pltpu.roll(f, 1, 0))
        return ahead - behind

    def curl(field, y, extra=None, comps=(0, 1, 2)):
        f = [field[c, y + 1] for c in comps]
        dy_x = field[comps[0], y + 2] - field[comps[0], y]
        dy_z = field[comps[2], y + 2] - field[comps[2], y]
        dz_x, dz_y = slope_z(f[0]), slope_z(f[1])
        if extra is not None:
            dz_x, dz_y = dz_x + extra[0], dz_y + extra[1]
        return (dy_z - dz_y, dz_x - slope_x(f[2]), slope_x(f[1]) - dy_x), f

    def each_row(body):
        for y in range(n):
            body(y)

    loads[1].wait()
    pltpu.make_async_copy(z_one.at[pl.ds(0, 2)], z_one.at[pl.ds(2, 2)], load_sem.at[3]).wait()
    loads[4].wait()

    def argument(y):
        turn, b = curl(bE, y)
        s = [v[c, y] for c in range(3)]
        sp = gE[SPREAD, y + 1] * (0.5 - 0.5 * (1.0 - iron_factor) * iron[y].astype(jnp.float32))
        gE[1, y + 1] = s[1] * b[2] - s[2] * b[1] - sp * turn[0]
        gE[0, y + 1] = s[2] * b[0] - s[0] * b[2] - sp * turn[1]
        gE[SPREAD, y + 1] = sp
        gE[3, y + 1] = s[0] * b[1] - s[1] * b[0] - sp * turn[2]

    each_row(argument)
    start(zg_moves)
    start(yg_moves)
    start(yc_moves)

    def local_solve(field, offset):
        def down(k, held):
            m = wide(m_tab[jnp.maximum(k - 1, 0)])
            rows = tuple(field[c, offset + k] + m * held[c] for c in range(3))
            for c in range(3):
                field[c, offset + k] = rows[c]
            return rows

        lax.fori_loop(0, n, down, (zero, zero, zero), unroll=True)

        def up(step, held):
            k = n - 1 - step
            m, inv = wide(m_tab[k]), wide(inv_tab[k])
            rows = tuple(field[c, offset + k] * inv + m * held[c] for c in range(3))
            for c in range(3):
                field[c, offset + k] = rows[c]
            return rows

        lax.fori_loop(0, n, up, (zero, zero, zero), unroll=True)

    left_gap, right_gap = 1.0 - s_low * aa, 1.0 - s_high * aa
    det = 1.0 / (left_gap * right_gap - s_low * s_high * cc * cc)
    ll, lr = right_gap * det, s_low * cc * det
    rr, rl = left_gap * det, s_high * cc * det
    mix[0] = ll * s_low
    mix[1] = lr * s_high
    mix[2] = rl * s_low
    mix[3] = rr * s_high
    low, high = one, one
    for k in range(1, groups):
        chain[0, k] = low
        chain[1, k] = high
        low = low * den_tab[jnp.maximum(me - k, 0)]
        high = high * den_tab[jnp.maximum(groups - 1 - me - k, 0)]
    for k in range(groups - 1):
        below = k < me
        reached = chain[jnp.where(below, 0, 1), jnp.where(below, me - k, k + 1 - me)]
        coef[0, k] = reached * jnp.where(below, ll, lr)
        coef[1, k] = reached * jnp.where(below, rl, rr)

    local_solve(wE, 1)

    def interface(slot, field, offset):
        first = [field[c, offset] for c in range(3)]
        last = [field[c, offset + n - 1] for c in range(3)]
        lefts, rights = [], []
        for c in range(3):
            left = wide(mix[0]) * first[c] + wide(mix[1]) * last[c]
            right = wide(mix[2]) * first[c] + wide(mix[3]) * last[c]
            for k in range(groups - 1):
                end = ends[slot, k, c]
                left = left + wide(coef[0, k]) * end
                right = right + wide(coef[1, k]) * end
            lefts.append(left)
            rights.append(right)
        return lefts, rights

    gather_all(0).wait_recv()
    lefts, rights = interface(0, wE, 1)
    for c in range(3):
        wE[c, 0] = lefts[c]
        wE[c, n + 1] = rights[c]

    def relax(y):
        near, far = wide(al_tab[y]), wide(al_tab[n - 1 - y])
        for c in range(3):
            wE[c, y + 1] = wE[c, y + 1] + near * wE[c, 0] + far * wE[c, n + 1]

    each_row(relax)
    start(zw_moves)

    def pull(y):
        turn, _ = curl(wE, y)
        sp = gE[SPREAD, y + 1]
        for c in range(3):
            tE[c, y] = turn[c]
            hE[c, y + 1] = sp * turn[c]

    each_row(pull)
    start(zh_moves)

    arrive(y_all + z_one_all)
    leave(y_all + z_one_all)

    for side, way in SIDES:
        have = (has_left, has_right)[side]
        edge, halo, y = (1, 0, 0) if side == 0 else (n, n + 1, n - 1)
        beyond, sp = way * y_one[side, NEAR_SPREAD], way * gE[SPREAD, edge]
        g_x = y_one[side, 4] + beyond * (bE[2, edge] + way * rim(yk[side, 0]))
        g_z = y_one[side, 6] - beyond * bE[0, edge]
        gE[1, halo] = jnp.where(have, g_x, 0.0)
        gE[3, halo] = jnp.where(have, g_z, 0.0)
        gE[1, edge] = gE[1, edge] - jnp.where(have, sp * y_one[side, 1], 0.0)
        gE[3, edge] = gE[3, edge] + jnp.where(have, sp * y_one[side, 0], 0.0)
        z_one[3, y] = z_one[3, y] - jnp.where(have, way * z_one[2 + SPREAD, y] * yk[side, 1], 0.0)

    def mend_argument(y):
        sp = gE[SPREAD, y + 1]
        gE[1, y + 1] = gE[1, y + 1] + sp * rim(z_one[1, y])
        gE[0, y + 1] = gE[0, y + 1] - sp * rim(z_one[0, y])

    each_row(mend_argument)

    totals = nothing
    for y in range(n):
        b = [bE[c, y + 1] for c in range(3)]
        sp = z_one[2 + SPREAD, y]
        extra = (
            jnp.where(active, sign * z_one[3, y] - sp * b[1], 0.0),
            jnp.where(active, sign * z_one[2, y] + sp * b[0], 0.0),
        )
        turn, _ = curl(gE, y, extra, G_COMPS)
        rows = [b[c] + half * turn[c] for c in range(3)]
        for c in range(3):
            new[c, y] = rows[c]
        totals = collect(totals, y, rows)
    put_sums(1, totals)
    for copy in gather(1):
        copy.start()

    def pull_field(y):
        turn = [tE[c, y] for c in range(3)]
        s = [v[c, y] for c in range(3)]
        adj[0, y] = wE[0, y + 1] + half * (turn[1] * s[2] - turn[2] * s[1])
        adj[1, y] = wE[1, y + 1] + half * (turn[2] * s[0] - turn[0] * s[2])
        adj[2, y] = wE[2, y + 1] + half * (turn[0] * s[1] - turn[1] * s[0])

    each_row(pull_field)
    wide_inv = wide(r_inv)
    for side, way in SIDES:
        have = (has_left, has_right)[side]
        edge, halo = (1, 0) if side == 0 else (n, n + 1)
        sp = y_one[side, NEAR_SPREAD]
        slope = {}
        for c in (0, 2):
            near, rim_row = wE[c, edge], wE[c, halo]
            outer = rim_row + (rim_row - near) + wide_inv * (rim_row - y_one[side, 2 + c // 2])
            slope[c] = way * (outer - near)
        cross = wE[1, halo]
        hE[0, halo] = jnp.where(have, sp * (slope[2] - slope_z(cross)), 0.0)
        hE[2, halo] = jnp.where(have, sp * (slope_x(cross) - slope[0]), 0.0)

    local_solve(new, 0)
    arrive(z_two_all)
    leave(z_two_all)

    for side, way in SIDES:
        have = (has_left, has_right)[side]
        halo = 0 if side == 0 else n + 1
        hE[0, halo] = hE[0, halo] - jnp.where(have, y_one[side, NEAR_SPREAD] * rim(z_two[1, halo]), 0.0)

    def mend_pull(y):
        c_x, c_y = rim(z_two[0, y + 1]), rim(z_two[1, y + 1])
        sp = gE[SPREAD, y + 1]
        s = [v[c, y] for c in range(3)]
        hE[0, y + 1] = hE[0, y + 1] - sp * c_y
        hE[1, y + 1] = hE[1, y + 1] + sp * c_x
        h_x, h_y = half * c_x, half * c_y
        adj[0, y] = adj[0, y] + h_x * s[2]
        adj[1, y] = adj[1, y] + h_y * s[2]
        adj[2, y] = adj[2, y] - (h_y * s[1] + h_x * s[0])

    each_row(mend_pull)

    def finish_adjoint(y):
        sp = z_one[2 + SPREAD, y]
        extra = (
            jnp.where(active, sign * z_two[0, n + 2 + y] + sp * wE[1, y + 1], 0.0),
            jnp.where(active, sign * z_two[1, n + 2 + y] - sp * wE[0, y + 1], 0.0),
        )
        turn, _ = curl(hE, y, extra)
        for c in range(3):
            adj[c, y] = adj[c, y] - half * turn[c]

    each_row(finish_adjoint)

    gather_all(1).wait_recv()
    lefts, rights = interface(1, new, 0)

    def finish(y):
        near, far = wide(al_tab[y]), wide(al_tab[n - 1 - y])
        for c in range(3):
            new[c, y] = new[c, y] + near * lefts[c] + far * rights[c]

    each_row(finish)

    for slot in range(2):
        gather_all(slot).wait_send()


def hand_over(new, adj, new_out, adj_out, sem):
    copies = [
        pltpu.make_async_copy(new, new_out, sem.at[0]),
        pltpu.make_async_copy(adj, adj_out, sem.at[1]),
    ]
    for copy in copies:
        copy.start()
    for copy in copies:
        copy.wait()


def local(groups, layers, magnetic, velocity, diffusivity, material, plane_rate, cotangent):
    _, n, nz, nx = magnetic.shape
    block = (3, n, nz, nx)
    rimmed = (3, n + 2, nz, nx)
    f32 = jnp.float32
    anywhere = pl.BlockSpec(memory_space=pl.ANY)
    inside = pl.BlockSpec(memory_space=pltpu.VMEM)
    args = [
        pltpu.with_memory_space_constraint(array, pltpu.HBM)
        for array in (magnetic, velocity, diffusivity, material, plane_rate.reshape(1, nz), cotangent)
    ]
    new, adj = pl.pallas_call(
        functools.partial(kernel, groups, layers, n),
        out_shape=[jax.ShapeDtypeStruct(block, f32)] * 2,
        in_specs=[anywhere] * 6,
        out_specs=[inside] * 2,
        scratch_shapes=[
            pltpu.VMEM(rimmed, f32),
            pltpu.VMEM((4, n + 2, nz, nx), f32),
            pltpu.VMEM(rimmed, f32),
            pltpu.VMEM(rimmed, f32),
            pltpu.VMEM(block, f32),
            pltpu.VMEM(block, f32),
            pltpu.VMEM((n, nz, nx), jnp.int32),
            pltpu.VMEM((1, nz), f32),
            pltpu.VMEM((5, n, nz, nx), f32),
            pltpu.VMEM((2, 2 * n + 2, nz, nx), f32),
            pltpu.VMEM((2, 7, nz, nx), f32),
            pltpu.VMEM((2, 2, nz, nx), f32),
            pltpu.VMEM((2, groups - 1, 3, nz, nx), f32),
            pltpu.VMEM((2, 2, 3, nz, nx), f32),
            pltpu.VMEM((n, nz, LANES), f32),
            pltpu.VMEM((n, nz, LANES), f32),
            pltpu.VMEM((n, nz, LANES), f32),
            pltpu.VMEM((groups, nz, LANES), f32),
            pltpu.VMEM((groups, nz, LANES), f32),
            pltpu.VMEM((2, n, nz, LANES), f32),
            pltpu.VMEM((4, nz, LANES), f32),
            pltpu.VMEM((2, groups - 1, nz, LANES), f32),
            pltpu.VMEM((2, groups, nz, LANES), f32),
            pltpu.SemaphoreType.DMA((5,)),
            pltpu.SemaphoreType.DMA((N_WAYS,)),
            pltpu.SemaphoreType.DMA((N_WAYS,)),
            pltpu.SemaphoreType.DMA((2,)),
            pltpu.SemaphoreType.DMA((2,)),
        ],
        compiler_params=pltpu.CompilerParams(
            collective_id=0, has_side_effects=True, vmem_limit_bytes=24 * 2**20
        ),
    )(*args)
    return tuple(pl.pallas_call(
        hand_over,
        out_shape=[jax.ShapeDtypeStruct(block, f32)] * 2,
        in_specs=[anywhere] * 2,
        out_specs=[anywhere] * 2,
        scratch_shapes=[pltpu.SemaphoreType.DMA((2,))],
        compiler_params=pltpu.CompilerParams(vmem_limit_bytes=2**20),
    )(new, adj))


def solution(mesh):
    in_specs = (
        P(None, "gy", "gz", None),
        P(None, "gy", "gz", None),
        P("gy", "gz", None),
        P("gy", "gz", None),
        P("gz"),
        P(None, "gy", "gz", None),
    )
    out_specs = (P(None, "gy", "gz", None), P(None, "gy", "gz", None))
    body = functools.partial(local, mesh.shape["gy"], mesh.shape["gz"])
    return jax.shard_map(body, mesh=mesh, in_specs=in_specs, out_specs=out_specs, check_vma=False)
```

```python
import functools
import jax
import jax.numpy as jnp
from jax import lax
from jax.experimental import pallas as pl
from jax.experimental.pallas import tpu as pltpu
from jax.sharding import PartitionSpec as P

step_size = 0.1
iron_factor = 0.2
MESH = pl.DeviceIdType.MESH
LANES = 128
SIDES = ((0, -1), (1, 1))
N_WAYS = 6
G_COMPS = (1, 0, 3)
SPREAD = 2
NEAR_SPREAD = 5


def kernel(
    groups, layers, n, mag, vel, dif, mat, rate, cot, new, adj, sides, al_tab,
    bE, gE, wE, hE, tE, v, iron, rate_row, z_one, z_two, y_one, yk, ends, sums,
    m_tab, inv_tab, s_tab, den_tab, w_tab, mix, coef, chain,
    load_sem, send_sem, recv_sem, gs_sem, gr_sem,
):
    me = lax.axis_index("gy")
    lay = lax.axis_index("gz")
    nx = bE.shape[-1]
    nz = bE.shape[-2]
    half = 0.5 * step_size

    rate_load = pltpu.make_async_copy(rate, rate_row, load_sem.at[4])
    rate_load.start()
    loads = [
        pltpu.make_async_copy(cot, wE.at[:, pl.ds(1, n)], load_sem.at[1]),
        pltpu.make_async_copy(mag, bE.at[:, pl.ds(1, n)], load_sem.at[0]),
        pltpu.make_async_copy(dif, gE.at[SPREAD, pl.ds(1, n)], load_sem.at[3]),
        pltpu.make_async_copy(mat, iron, load_sem.at[3]),
        pltpu.make_async_copy(vel, v, load_sem.at[2]),
    ]
    for load in loads:
        load.start()

    has_left, has_right = me > 0, me < groups - 1
    has_low, has_high = lay > 0, lay < layers - 1

    def there(dy, dz):
        found = None
        for step, low, high in ((dy, has_left, has_right), (dz, has_low, has_high)):
            if step:
                seen = low if step < 0 else high
                found = seen if found is None else jnp.logical_and(found, seen)
        return found

    def place(dy, dz):
        return {
            "gy": jnp.clip(me + dy, 0, groups - 1) if dy else me,
            "gz": jnp.clip(lay + dz, 0, layers - 1) if dz else lay,
        }

    around = [(dy, dz) for dy in (-1, 0, 1) for dz in (-1, 0, 1) if dz]
    barrier = pltpu.get_barrier_semaphore()
    for k in range(1, groups):
        pl.semaphore_signal(
            barrier, inc=1, device_id={"gy": lax.rem(me + k, groups), "gz": lay}, device_id_type=MESH
        )
    count = jnp.int32(groups - 1)
    for dy, dz in around:
        count = count + there(dy, dz).astype(jnp.int32)

        @pl.when(there(dy, dz))
        def _():
            pl.semaphore_signal(barrier, inc=1, device_id=place(dy, dz), device_id_type=MESH)

    def move(slot, src, dst, dy, dz):
        copy = pltpu.make_async_remote_copy(
            src_ref=src, dst_ref=dst, send_sem=send_sem.at[slot], recv_sem=recv_sem.at[slot],
            device_id=place(dy, dz), device_id_type=MESH)
        return copy, there(dy, dz), there(-dy, -dz)

    def start(moves):
        for copy, ahead, _ in moves:
            @pl.when(ahead)
            def _():
                copy.start()

    def arrive(moves):
        for copy, _, behind in moves:
            @pl.when(behind)
            def _():
                copy.wait_recv()

    def leave(moves):
        for copy, ahead, _ in moves:
            @pl.when(ahead)
            def _():
                copy.wait_send()

    Y_WAYS = ((-1, 0, 1), (1, n - 1, 0))
    Z_WAYS = ((-1, 0, nz - 1), (1, nz - 1, 0))

    def y_moves(slot, src, dst, first):
        return [
            move(slot + i, src(first + row), dst(side), dy, 0)
            for i, (dy, row, side) in enumerate(Y_WAYS)
        ]

    def z_moves(slot, src, dst):
        return [
            move(slot + i, src(pl.ds(mine, 1)), dst(pl.ds(theirs, 1)), 0, dz)
            for i, (dz, mine, theirs) in enumerate(Z_WAYS)
        ]

    yb_moves = [
        copy for i, c in enumerate((0, 2))
        for copy in y_moves(0, lambda row: mag.at[c, row], lambda side: y_one.at[side, i], 0)
    ]
    yc_moves = [
        copy for i, c in enumerate((0, 2))
        for copy in y_moves(0, lambda row: cot.at[c, row], lambda side: y_one.at[side, 2 + i], 0)
    ]
    yg_moves = y_moves(0, lambda row: gE.at[pl.ds(1, 3), row], lambda side: y_one.at[side, pl.ds(4, 3)], 1)
    yk_moves = [
        move(
            i, mag.at[pl.ds(1, 2), row, pl.ds(mine, 1)], yk.at[side, :, pl.ds(theirs, 1)], dy, dz
        )
        for i, (dy, row, side) in enumerate(Y_WAYS)
        for j, (dz, mine, theirs) in enumerate(Z_WAYS)
    ]
    both = pl.ds(0, 2)
    w_rows, h_rows = pl.ds(0, n + 2), pl.ds(n + 2, n)
    zb_moves = z_moves(2, lambda z: mag.at[both, :, z], lambda z: z_one.at[both, :, z])
    cut = n // 2
    zg_moves, zg_rest = (
        z_moves(
            2,
            lambda z: gE.at[pl.ds(0, 3), pl.ds(1 + first, rows), z],
            lambda z: z_one.at[pl.ds(2, 3), pl.ds(first, rows), z],
        )
        for first, rows in ((0, cut), (cut, n - cut))
    )
    z_one_all = [
        move(2 + i, z_one.at[:, :, pl.ds(theirs, 1)], z_one.at[:, :, pl.ds(theirs, 1)], 0, dz)
        for i, (dz, _, theirs) in enumerate(Z_WAYS)
    ]
    layers_by = has_low.astype(jnp.int32) + has_high.astype(jnp.int32)
    y_all = []
    for i, (dy, _, _) in enumerate(Y_WAYS):
        for by in range(3):
            rows = z_two.at[:, pl.ds(0, 7 * nz // 2 + by), pl.ds(0, 1)]
            copy, ahead, behind = move(i, rows, rows, dy, 0)
            fits = layers_by == by
            y_all.append((copy, jnp.logical_and(ahead, fits), jnp.logical_and(behind, fits)))
    zw_moves = z_moves(4, lambda z: wE.at[both, :, z], lambda z: z_two.at[:, w_rows, z])
    zh_moves = z_moves(4, lambda z: hE.at[both, pl.ds(1, n), z], lambda z: z_two.at[:, h_rows, z])
    z_two_all = [
        move(4 + i, z_two.at[:, :, pl.ds(theirs, 1)], z_two.at[:, :, pl.ds(theirs, 1)], 0, dz)
        for i, (dz, _, theirs) in enumerate(Z_WAYS)
    ]

    zero = jnp.zeros((nz, nx), jnp.float32)
    for part in (0, 2):
        bE[part, 0] = zero
        bE[part, n + 1] = zero

    def wide(tile):
        return jnp.concatenate([tile] * (nx // LANES), axis=1)

    lane = lax.broadcasted_iota(jnp.int32, (nz, LANES), 1)
    sub = wide(lax.broadcasted_iota(jnp.int32, (nz, LANES), 0))
    flag = jnp.where(
        sub == nz - 1, has_high.astype(jnp.int32), jnp.where(sub == 0, has_low.astype(jnp.int32), 0)
    )
    active = flag > 0
    sign = jnp.where(sub == 0, -1.0, 1.0)

    def rim(halo):
        return jnp.where(active, sign * halo, 0.0)

    square = (
        lax.broadcasted_iota(jnp.int32, (nz, nz), 0) == lax.broadcasted_iota(jnp.int32, (nz, nz), 1)
    )
    rate_load.wait()
    r = jnp.sum(jnp.where(square, jnp.broadcast_to(rate_row[...], (nz, nz)), 0.0), axis=1, keepdims=True)
    r = jnp.broadcast_to(r, (nz, LANES))
    one = jnp.ones((nz, LANES), jnp.float32)

    r_inv = 1.0 / r
    whole, grown = one, one
    sizes = [one]
    for k in range(n):
        grown = grown + r_inv * whole
        whole = whole + grown
        sizes.append(whole)
    full_inv = 1.0 / whole
    for k in range(n):
        m = sizes[k] / sizes[k + 1]
        m_tab[k] = m
        inv_tab[k] = m * r_inv
        al_tab[n - 1 - k] = sizes[k] * full_inv
    aa, cc = sizes[n - 1] * full_inv, full_inv

    def reach(k, s):
        s_tab[k] = s
        den = cc / (1.0 - s * aa)
        den_tab[k] = den
        return aa + cc * s * den

    lax.fori_loop(0, groups, reach, jnp.zeros((nz, LANES), jnp.float32), unroll=groups <= 8)
    s_low, s_high = s_tab[me], s_tab[groups - 1 - me]
    from_low, from_high = den_tab[me] * s_low, den_tab[groups - 1 - me] * s_high
    for k in range(n):
        near, far = al_tab[k] * r_inv, al_tab[n - 1 - k] * r_inv
        w_tab[0, k] = far + from_low * near
        w_tab[1, k] = near + from_high * far

    def gather(slot):
        copies = []
        for k in range(groups - 1):
            above = (me <= k).astype(jnp.int32)
            partner = k + above
            copies.append(pltpu.make_async_remote_copy(
                src_ref=sums.at[slot, 1 - above], dst_ref=ends.at[slot, me - 1 + above],
                send_sem=gs_sem.at[slot], recv_sem=gr_sem.at[slot],
                device_id={"gy": partner, "gz": lay}, device_id_type=MESH,
            ))
        return copies

    def gather_all(slot):
        return pltpu.make_async_remote_copy(
            src_ref=ends.at[slot], dst_ref=ends.at[slot], send_sem=gs_sem.at[slot], recv_sem=gr_sem.at[slot],
            device_id={"gy": lax.rem(me + 1, groups), "gz": lay}, device_id_type=MESH)

    nothing = (zero,) * 6

    def collect(totals, k, rows):
        toward = (wide(w_tab[0, k]), wide(w_tab[1, k]))
        return tuple(totals[3 * way + c] + toward[way] * rows[c] for way in range(2) for c in range(3))

    def put_sums(slot, totals):
        for way in range(2):
            for c in range(3):
                sums[slot, way, c] = totals[3 * way + c]

    loads[0].wait()
    totals = nothing
    for k in range(n):
        totals = collect(totals, k, [wE[c, k + 1] for c in range(3)])
    put_sums(0, totals)

    pl.semaphore_wait(barrier, count)
    start(yk_moves)
    for copy in gather(0):
        copy.start()
    start(zb_moves)
    start(yb_moves)

    def slope_x(f):
        tiles = [f[:, at:at + LANES] for at in range(0, nx, LANES)]
        ahead = [pltpu.roll(tile, LANES - 1, 1) for tile in tiles] + [jnp.zeros_like(tiles[0])]
        behind = [jnp.zeros_like(tiles[0])] + [pltpu.roll(tile, 1, 1) for tile in tiles]
        return jnp.concatenate(
            [
                jnp.where(lane == LANES - 1, ahead[t + 1], ahead[t])
                - jnp.where(lane == 0, behind[t], behind[t + 1])
                for t in range(len(tiles))
            ],
            axis=1,
        )

    def slope_z(f):
        ahead = jnp.where(sub == nz - 1, 0.0, pltpu.roll(f, nz - 1, 0))
        behind = jnp.where(sub == 0, 0.0, pltpu.roll(f, 1, 0))
        return ahead - behind

    def curl(field, y, extra=None, comps=(0, 1, 2)):
        f = [field[c, y + 1] for c in comps]
        dy_x = field[comps[0], y + 2] - field[comps[0], y]
        dy_z = field[comps[2], y + 2] - field[comps[2], y]
        dz_x, dz_y = slope_z(f[0]), slope_z(f[1])
        if extra is not None:
            dz_x, dz_y = dz_x + extra[0], dz_y + extra[1]
        return (dy_z - dz_y, dz_x - slope_x(f[2]), slope_x(f[1]) - dy_x), f

    def each_row(body):
        for y in range(n):
            body(y)

    loads[1].wait()
    pltpu.make_async_copy(z_one.at[pl.ds(0, 2)], z_one.at[pl.ds(2, 2)], load_sem.at[3]).wait()
    loads[4].wait()

    def argument(y):
        turn, b = curl(bE, y)
        s = [v[c, y] for c in range(3)]
        sp = gE[SPREAD, y + 1] * (0.5 - 0.5 * (1.0 - iron_factor) * iron[y].astype(jnp.float32))
        gE[1, y + 1] = s[1] * b[2] - s[2] * b[1] - sp * turn[0]
        gE[0, y + 1] = s[2] * b[0] - s[0] * b[2] - sp * turn[1]
        gE[SPREAD, y + 1] = sp
        gE[3, y + 1] = s[0] * b[1] - s[1] * b[0] - sp * turn[2]

    for y in range(cut):
        argument(y)
    start(zg_moves)
    for y in range(cut, n):
        argument(y)
    start(zg_rest)
    start(yg_moves)
    start(yc_moves)

    def local_solve(field, offset):
        def down(k, held):
            m = wide(m_tab[jnp.maximum(k - 1, 0)])
            rows = tuple(field[c, offset + k] + m * held[c] for c in range(3))
            for c in range(3):
                field[c, offset + k] = rows[c]
            return rows

        lax.fori_loop(0, n, down, (zero, zero, zero), unroll=True)

        def up(step, held):
            k = n - 1 - step
            m, inv = wide(m_tab[k]), wide(inv_tab[k])
            rows = tuple(field[c, offset + k] * inv + m * held[c] for c in range(3))
            for c in range(3):
                field[c, offset + k] = rows[c]
            return rows

        lax.fori_loop(0, n, up, (zero, zero, zero), unroll=True)

    left_gap, right_gap = 1.0 - s_low * aa, 1.0 - s_high * aa
    det = 1.0 / (left_gap * right_gap - s_low * s_high * cc * cc)
    ll, lr = right_gap * det, s_low * cc * det
    rr, rl = left_gap * det, s_high * cc * det
    mix[0] = ll * s_low
    mix[1] = lr * s_high
    mix[2] = rl * s_low
    mix[3] = rr * s_high
    low, high = one, one
    for k in range(1, groups):
        chain[0, k] = low
        chain[1, k] = high
        low = low * den_tab[jnp.maximum(me - k, 0)]
        high = high * den_tab[jnp.maximum(groups - 1 - me - k, 0)]
    for k in range(groups - 1):
        below = k < me
        reached = chain[jnp.where(below, 0, 1), jnp.where(below, me - k, k + 1 - me)]
        coef[0, k] = reached * jnp.where(below, ll, lr)
        coef[1, k] = reached * jnp.where(below, rl, rr)

    local_solve(wE, 1)

    def interface(slot, field, offset):
        first = [field[c, offset] for c in range(3)]
        last = [field[c, offset + n - 1] for c in range(3)]
        lefts, rights = [], []
        for c in range(3):
            left = wide(mix[0]) * first[c] + wide(mix[1]) * last[c]
            right = wide(mix[2]) * first[c] + wide(mix[3]) * last[c]
            for k in range(groups - 1):
                end = ends[slot, k, c]
                left = left + wide(coef[0, k]) * end
                right = right + wide(coef[1, k]) * end
            lefts.append(left)
            rights.append(right)
        return lefts, rights

    gather_all(0).wait_recv()
    lefts, rights = interface(0, wE, 1)
    for c in range(3):
        wE[c, 0] = lefts[c]
        wE[c, n + 1] = rights[c]

    def relax(y):
        near, far = wide(al_tab[y]), wide(al_tab[n - 1 - y])
        for c in range(3):
            wE[c, y + 1] = wE[c, y + 1] + near * wE[c, 0] + far * wE[c, n + 1]

    each_row(relax)
    start(zw_moves)

    def pull(y):
        turn, _ = curl(wE, y)
        sp = gE[SPREAD, y + 1]
        for c in range(3):
            tE[c, y] = turn[c]
            hE[c, y + 1] = sp * turn[c]

    each_row(pull)
    start(zh_moves)

    arrive(y_all + z_one_all)
    leave(y_all + z_one_all)

    for side, way in SIDES:
        have = (has_left, has_right)[side]
        edge, halo, y = (1, 0, 0) if side == 0 else (n, n + 1, n - 1)
        beyond, sp = way * y_one[side, NEAR_SPREAD], way * gE[SPREAD, edge]
        g_x = y_one[side, 4] + beyond * (bE[2, edge] + way * rim(yk[side, 0]))
        g_z = y_one[side, 6] - beyond * bE[0, edge]
        gE[1, halo] = jnp.where(have, g_x, 0.0)
        gE[3, halo] = jnp.where(have, g_z, 0.0)
        gE[1, edge] = gE[1, edge] - jnp.where(have, sp * y_one[side, 1], 0.0)
        gE[3, edge] = gE[3, edge] + jnp.where(have, sp * y_one[side, 0], 0.0)
        z_one[3, y] = z_one[3, y] - jnp.where(have, way * z_one[2 + SPREAD, y] * yk[side, 1], 0.0)

    def mend_argument(y):
        sp = gE[SPREAD, y + 1]
        gE[1, y + 1] = gE[1, y + 1] + sp * rim(z_one[1, y])
        gE[0, y + 1] = gE[0, y + 1] - sp * rim(z_one[0, y])

    each_row(mend_argument)

    totals = nothing
    for y in range(n):
        b = [bE[c, y + 1] for c in range(3)]
        sp = z_one[2 + SPREAD, y]
        extra = (
            jnp.where(active, sign * z_one[3, y] - sp * b[1], 0.0),
            jnp.where(active, sign * z_one[2, y] + sp * b[0], 0.0),
        )
        turn, _ = curl(gE, y, extra, G_COMPS)
        rows = [b[c] + half * turn[c] for c in range(3)]
        for c in range(3):
            new[c, y] = rows[c]
        totals = collect(totals, y, rows)
    put_sums(1, totals)
    for copy in gather(1):
        copy.start()

    def pull_field(y):
        turn = [tE[c, y] for c in range(3)]
        s = [v[c, y] for c in range(3)]
        adj[0, y] = wE[0, y + 1] + half * (turn[1] * s[2] - turn[2] * s[1])
        adj[1, y] = wE[1, y + 1] + half * (turn[2] * s[0] - turn[0] * s[2])
        adj[2, y] = wE[2, y + 1] + half * (turn[0] * s[1] - turn[1] * s[0])

    each_row(pull_field)
    wide_inv = wide(r_inv)
    for side, way in SIDES:
        have = (has_left, has_right)[side]
        edge, halo = (1, 0) if side == 0 else (n, n + 1)
        sp = y_one[side, NEAR_SPREAD]
        slope = {}
        for c in (0, 2):
            near, rim_row = wE[c, edge], wE[c, halo]
            outer = rim_row + (rim_row - near) + wide_inv * (rim_row - y_one[side, 2 + c // 2])
            slope[c] = way * (outer - near)
        cross = wE[1, halo]
        hE[0, halo] = jnp.where(have, sp * (slope[2] - slope_z(cross)), 0.0)
        hE[2, halo] = jnp.where(have, sp * (slope_x(cross) - slope[0]), 0.0)

    local_solve(new, 0)
    arrive(z_two_all)
    leave(z_two_all)

    for side, way in SIDES:
        have = (has_left, has_right)[side]
        halo = 0 if side == 0 else n + 1
        hE[0, halo] = hE[0, halo] - jnp.where(have, y_one[side, NEAR_SPREAD] * rim(z_two[1, halo]), 0.0)

    def mend_pull(y):
        c_x, c_y = rim(z_two[0, y + 1]), rim(z_two[1, y + 1])
        sp = gE[SPREAD, y + 1]
        s = [v[c, y] for c in range(3)]
        hE[0, y + 1] = hE[0, y + 1] - sp * c_y
        hE[1, y + 1] = hE[1, y + 1] + sp * c_x
        h_x, h_y = half * c_x, half * c_y
        adj[0, y] = adj[0, y] + h_x * s[2]
        adj[1, y] = adj[1, y] + h_y * s[2]
        adj[2, y] = adj[2, y] - (h_y * s[1] + h_x * s[0])

    each_row(mend_pull)

    def finish_adjoint(y):
        sp = z_one[2 + SPREAD, y]
        extra = (
            jnp.where(active, sign * z_two[0, n + 2 + y] + sp * wE[1, y + 1], 0.0),
            jnp.where(active, sign * z_two[1, n + 2 + y] - sp * wE[0, y + 1], 0.0),
        )
        turn, _ = curl(hE, y, extra)
        for c in range(3):
            adj[c, y] = adj[c, y] - half * turn[c]

    each_row(finish_adjoint)

    gather_all(1).wait_recv()
    lefts, rights = interface(1, new, 0)
    for c in range(3):
        sides[0, c] = lefts[c]
        sides[1, c] = rights[c]

    for slot in range(2):
        gather_all(slot).wait_send()


def hand_over(new, adj, sides, al_tab, new_out, adj_out, done, sem):
    n, nx = done.shape[1], done.shape[3]
    step = 12 if n % 12 == 0 else n
    adj_copy = pltpu.make_async_copy(adj, adj_out, sem.at[0])
    adj_copy.start()
    copies = []
    for first in range(0, n, step):
        for y in range(first, first + step):
            near, far = (jnp.concatenate([al_tab[k]] * (nx // LANES), axis=1) for k in (y, n - 1 - y))
            for c in range(3):
                done[c, y] = new[c, y] + near * sides[0, c] + far * sides[1, c]
        rows = pl.ds(first, step)
        copies.append(pltpu.make_async_copy(done.at[:, rows], new_out.at[:, rows], sem.at[1 + first // step]))
        copies[-1].start()
    for copy in copies:
        copy.wait()
    adj_copy.wait()


def local(groups, layers, magnetic, velocity, diffusivity, material, plane_rate, cotangent):
    _, n, nz, nx = magnetic.shape
    block = (3, n, nz, nx)
    rimmed = (3, n + 2, nz, nx)
    f32 = jnp.float32
    anywhere = pl.BlockSpec(memory_space=pl.ANY)
    inside = pl.BlockSpec(memory_space=pltpu.VMEM)
    args = [
        pltpu.with_memory_space_constraint(array, pltpu.HBM)
        for array in (magnetic, velocity, diffusivity, material, plane_rate.reshape(1, nz), cotangent)
    ]
    parts = pl.pallas_call(
        functools.partial(kernel, groups, layers, n),
        out_shape=[
            jax.ShapeDtypeStruct(block, f32),
            jax.ShapeDtypeStruct(block, f32),
            jax.ShapeDtypeStruct((2, 3, nz, nx), f32),
            jax.ShapeDtypeStruct((n, nz, LANES), f32),
        ],
        in_specs=[anywhere] * 6,
        out_specs=[inside] * 4,
        scratch_shapes=[
            pltpu.VMEM(rimmed, f32),
            pltpu.VMEM((4, n + 2, nz, nx), f32),
            pltpu.VMEM(rimmed, f32),
            pltpu.VMEM(rimmed, f32),
            pltpu.VMEM(block, f32),
            pltpu.VMEM(block, f32),
            pltpu.VMEM((n, nz, nx), jnp.int32),
            pltpu.VMEM((1, nz), f32),
            pltpu.VMEM((5, n, nz, nx), f32),
            pltpu.VMEM((2, 2 * n + 2, nz, nx), f32),
            pltpu.VMEM((2, 7, nz, nx), f32),
            pltpu.VMEM((2, 2, nz, nx), f32),
            pltpu.VMEM((2, groups - 1, 3, nz, nx), f32),
            pltpu.VMEM((2, 2, 3, nz, nx), f32),
            pltpu.VMEM((n, nz, LANES), f32),
            pltpu.VMEM((n, nz, LANES), f32),
            pltpu.VMEM((groups, nz, LANES), f32),
            pltpu.VMEM((groups, nz, LANES), f32),
            pltpu.VMEM((2, n, nz, LANES), f32),
            pltpu.VMEM((4, nz, LANES), f32),
            pltpu.VMEM((2, groups - 1, nz, LANES), f32),
            pltpu.VMEM((2, groups, nz, LANES), f32),
            pltpu.SemaphoreType.DMA((5,)),
            pltpu.SemaphoreType.DMA((N_WAYS,)),
            pltpu.SemaphoreType.DMA((N_WAYS,)),
            pltpu.SemaphoreType.DMA((2,)),
            pltpu.SemaphoreType.DMA((2,)),
        ],
        compiler_params=pltpu.CompilerParams(
            collective_id=0, has_side_effects=True, vmem_limit_bytes=24 * 2**20
        ),
    )(*args)
    return tuple(pl.pallas_call(
        hand_over,
        out_shape=[jax.ShapeDtypeStruct(block, f32)] * 2,
        in_specs=[inside] * 4,
        out_specs=[anywhere] * 2,
        scratch_shapes=[pltpu.VMEM(block, f32), pltpu.SemaphoreType.DMA((3,))],
        compiler_params=pltpu.CompilerParams(vmem_limit_bytes=2 * 2**20),
    )(*parts))


def solution(mesh):
    in_specs = (
        P(None, "gy", "gz", None),
        P(None, "gy", "gz", None),
        P("gy", "gz", None),
        P("gy", "gz", None),
        P("gz"),
        P(None, "gy", "gz", None),
    )
    out_specs = (P(None, "gy", "gz", None), P(None, "gy", "gz", None))
    body = functools.partial(local, mesh.shape["gy"], mesh.shape["gz"])
    return jax.shard_map(body, mesh=mesh, in_specs=in_specs, out_specs=out_specs, check_vma=False)
```

```python
import functools
import jax
import jax.numpy as jnp
from jax import lax
from jax.experimental import pallas as pl
from jax.experimental.pallas import tpu as pltpu
from jax.sharding import PartitionSpec as P

step_size = 0.1
iron_factor = 0.2
MESH = pl.DeviceIdType.MESH
LANES = 128
SIDES = ((0, -1), (1, 1))
N_WAYS = 6
G_COMPS = (1, 0, 3)
SPREAD = 2
NEAR_SPREAD = 5


def kernel(
    groups, layers, n, mag, vel, dif, mat, rate, cot, new, adj, sides, al_tab,
    bE, gE, wE, hE, tE, v, iron, rate_row, z_one, z_two, y_one, yk, ends, sums,
    m_tab, inv_tab, s_tab, den_tab, w_tab, mix, coef, chain,
    load_sem, send_sem, recv_sem, gs_sem, gr_sem,
):
    me = lax.axis_index("gy")
    lay = lax.axis_index("gz")
    nx = bE.shape[-1]
    nz = bE.shape[-2]
    half = 0.5 * step_size

    rate_load = pltpu.make_async_copy(rate, rate_row, load_sem.at[4])
    rate_load.start()
    loads = [
        pltpu.make_async_copy(cot, wE.at[:, pl.ds(1, n)], load_sem.at[1]),
        pltpu.make_async_copy(mag, bE.at[:, pl.ds(1, n)], load_sem.at[0]),
        pltpu.make_async_copy(dif, gE.at[SPREAD, pl.ds(1, n)], load_sem.at[3]),
        pltpu.make_async_copy(mat, iron, load_sem.at[3]),
        pltpu.make_async_copy(vel, v, load_sem.at[2]),
    ]
    for load in loads:
        load.start()

    has_left, has_right = me > 0, me < groups - 1
    has_low, has_high = lay > 0, lay < layers - 1

    def there(dy, dz):
        found = None
        for step, low, high in ((dy, has_left, has_right), (dz, has_low, has_high)):
            if step:
                seen = low if step < 0 else high
                found = seen if found is None else jnp.logical_and(found, seen)
        return found

    def place(dy, dz):
        return {
            "gy": jnp.clip(me + dy, 0, groups - 1) if dy else me,
            "gz": jnp.clip(lay + dz, 0, layers - 1) if dz else lay,
        }

    around = [(dy, dz) for dy in (-1, 0, 1) for dz in (-1, 0, 1) if dz]
    barrier = pltpu.get_barrier_semaphore()
    for k in range(1, groups):
        pl.semaphore_signal(
            barrier, inc=1, device_id={"gy": lax.rem(me + k, groups), "gz": lay}, device_id_type=MESH
        )
    count = jnp.int32(groups - 1)
    for dy, dz in around:
        count = count + there(dy, dz).astype(jnp.int32)

        @pl.when(there(dy, dz))
        def _():
            pl.semaphore_signal(barrier, inc=1, device_id=place(dy, dz), device_id_type=MESH)

    def move(slot, src, dst, dy, dz):
        copy = pltpu.make_async_remote_copy(
            src_ref=src, dst_ref=dst, send_sem=send_sem.at[slot], recv_sem=recv_sem.at[slot],
            device_id=place(dy, dz), device_id_type=MESH)
        return copy, there(dy, dz), there(-dy, -dz)

    def start(moves):
        for copy, ahead, _ in moves:
            @pl.when(ahead)
            def _():
                copy.start()

    def arrive(moves):
        for copy, _, behind in moves:
            @pl.when(behind)
            def _():
                copy.wait_recv()

    def leave(moves):
        for copy, ahead, _ in moves:
            @pl.when(ahead)
            def _():
                copy.wait_send()

    Y_WAYS = ((-1, 0, 1), (1, n - 1, 0))
    Z_WAYS = ((-1, 0, nz - 1), (1, nz - 1, 0))

    def y_moves(slot, src, dst, first):
        return [
            move(slot + i, src(first + row), dst(side), dy, 0)
            for i, (dy, row, side) in enumerate(Y_WAYS)
        ]

    def z_moves(slot, src, dst):
        return [
            move(slot + i, src(pl.ds(mine, 1)), dst(pl.ds(theirs, 1)), 0, dz)
            for i, (dz, mine, theirs) in enumerate(Z_WAYS)
        ]

    yb_moves = [
        copy for i, c in enumerate((0, 2))
        for copy in y_moves(0, lambda row: mag.at[c, row], lambda side: y_one.at[side, i], 0)
    ]
    yc_moves = [
        copy for i, c in enumerate((0, 2))
        for copy in y_moves(0, lambda row: cot.at[c, row], lambda side: y_one.at[side, 2 + i], 0)
    ]
    yg_moves = y_moves(0, lambda row: gE.at[pl.ds(1, 3), row], lambda side: y_one.at[side, pl.ds(4, 3)], 1)
    yk_moves = [
        move(
            i, mag.at[pl.ds(1, 2), row, pl.ds(mine, 1)], yk.at[side, :, pl.ds(theirs, 1)], dy, dz
        )
        for i, (dy, row, side) in enumerate(Y_WAYS)
        for j, (dz, mine, theirs) in enumerate(Z_WAYS)
    ]
    both = pl.ds(0, 2)
    w_rows, h_rows = pl.ds(0, n + 2), pl.ds(n + 2, n)
    zb_moves = z_moves(2, lambda z: mag.at[both, :, z], lambda z: z_one.at[both, :, z])
    cut = n // 2
    zg_moves, zg_rest = (
        z_moves(
            2,
            lambda z: gE.at[pl.ds(0, 3), pl.ds(1 + first, rows), z],
            lambda z: z_one.at[pl.ds(2, 3), pl.ds(first, rows), z],
        )
        for first, rows in ((0, cut), (cut, n - cut))
    )
    z_one_all = [
        move(2 + i, z_one.at[:, :, pl.ds(theirs, 1)], z_one.at[:, :, pl.ds(theirs, 1)], 0, dz)
        for i, (dz, _, theirs) in enumerate(Z_WAYS)
    ]
    layers_by = has_low.astype(jnp.int32) + has_high.astype(jnp.int32)
    y_all = []
    for i, (dy, _, _) in enumerate(Y_WAYS):
        for by in range(3):
            rows = z_two.at[:, pl.ds(0, 7 * nz // 2 + by), pl.ds(0, 1)]
            copy, ahead, behind = move(i, rows, rows, dy, 0)
            fits = layers_by == by
            y_all.append((copy, jnp.logical_and(ahead, fits), jnp.logical_and(behind, fits)))
    zw_moves = z_moves(4, lambda z: wE.at[both, :, z], lambda z: z_two.at[:, w_rows, z])
    zh_moves = z_moves(4, lambda z: hE.at[both, pl.ds(1, n), z], lambda z: z_two.at[:, h_rows, z])
    z_two_all = [
        move(4 + i, z_two.at[:, :, pl.ds(theirs, 1)], z_two.at[:, :, pl.ds(theirs, 1)], 0, dz)
        for i, (dz, _, theirs) in enumerate(Z_WAYS)
    ]

    zero = jnp.zeros((nz, nx), jnp.float32)
    for part in (0, 2):
        bE[part, 0] = zero
        bE[part, n + 1] = zero

    def wide(tile):
        return jnp.concatenate([tile] * (nx // LANES), axis=1)

    lane = lax.broadcasted_iota(jnp.int32, (nz, LANES), 1)
    sub = wide(lax.broadcasted_iota(jnp.int32, (nz, LANES), 0))
    flag = jnp.where(
        sub == nz - 1, has_high.astype(jnp.int32), jnp.where(sub == 0, has_low.astype(jnp.int32), 0)
    )
    active = flag > 0
    sign = jnp.where(sub == 0, -1.0, 1.0)

    def rim(halo):
        return jnp.where(active, sign * halo, 0.0)

    square = (
        lax.broadcasted_iota(jnp.int32, (nz, nz), 0) == lax.broadcasted_iota(jnp.int32, (nz, nz), 1)
    )
    rate_load.wait()
    r = jnp.sum(jnp.where(square, jnp.broadcast_to(rate_row[...], (nz, nz)), 0.0), axis=1, keepdims=True)
    r = jnp.broadcast_to(r, (nz, LANES))
    one = jnp.ones((nz, LANES), jnp.float32)

    r_inv = 1.0 / r
    whole, grown = one, one
    sizes = [one]
    for k in range(n):
        grown = grown + r_inv * whole
        whole = whole + grown
        sizes.append(whole)
    full_inv = 1.0 / whole
    for k in range(n):
        m = sizes[k] / sizes[k + 1]
        m_tab[k] = m
        inv_tab[k] = m * r_inv
        al_tab[n - 1 - k] = sizes[k] * full_inv
    aa, cc = sizes[n - 1] * full_inv, full_inv

    def reach(k, s):
        s_tab[k] = s
        den = cc / (1.0 - s * aa)
        den_tab[k] = den
        return aa + cc * s * den

    lax.fori_loop(0, groups, reach, jnp.zeros((nz, LANES), jnp.float32), unroll=groups <= 8)
    s_low, s_high = s_tab[me], s_tab[groups - 1 - me]
    from_low, from_high = den_tab[me] * s_low, den_tab[groups - 1 - me] * s_high
    for k in range(n):
        near, far = al_tab[k] * r_inv, al_tab[n - 1 - k] * r_inv
        w_tab[0, k] = far + from_low * near
        w_tab[1, k] = near + from_high * far

    def gather(slot):
        copies = []
        for k in range(groups - 1):
            above = (me <= k).astype(jnp.int32)
            partner = k + above
            copies.append(pltpu.make_async_remote_copy(
                src_ref=sums.at[slot, 1 - above], dst_ref=ends.at[slot, me - 1 + above],
                send_sem=gs_sem.at[slot], recv_sem=gr_sem.at[slot],
                device_id={"gy": partner, "gz": lay}, device_id_type=MESH,
            ))
        return copies

    def gather_all(slot):
        return pltpu.make_async_remote_copy(
            src_ref=ends.at[slot], dst_ref=ends.at[slot], send_sem=gs_sem.at[slot], recv_sem=gr_sem.at[slot],
            device_id={"gy": lax.rem(me + 1, groups), "gz": lay}, device_id_type=MESH)

    nothing = (zero,) * 6

    def collect(totals, k, rows):
        toward = (wide(w_tab[0, k]), wide(w_tab[1, k]))
        return tuple(totals[3 * way + c] + toward[way] * rows[c] for way in range(2) for c in range(3))

    def put_sums(slot, totals):
        for way in range(2):
            for c in range(3):
                sums[slot, way, c] = totals[3 * way + c]

    loads[0].wait()
    totals = nothing
    for k in range(n):
        totals = collect(totals, k, [wE[c, k + 1] for c in range(3)])
    put_sums(0, totals)

    pl.semaphore_wait(barrier, count)
    start(yk_moves)
    for copy in gather(0):
        copy.start()
    start(zb_moves)
    start(yb_moves)

    def slope_x(f):
        tiles = [f[:, at:at + LANES] for at in range(0, nx, LANES)]
        ahead = [pltpu.roll(tile, LANES - 1, 1) for tile in tiles] + [jnp.zeros_like(tiles[0])]
        behind = [jnp.zeros_like(tiles[0])] + [pltpu.roll(tile, 1, 1) for tile in tiles]
        return jnp.concatenate(
            [
                jnp.where(lane == LANES - 1, ahead[t + 1], ahead[t])
                - jnp.where(lane == 0, behind[t], behind[t + 1])
                for t in range(len(tiles))
            ],
            axis=1,
        )

    def slope_z(f):
        ahead = jnp.where(sub == nz - 1, 0.0, pltpu.roll(f, nz - 1, 0))
        behind = jnp.where(sub == 0, 0.0, pltpu.roll(f, 1, 0))
        return ahead - behind

    def curl(field, y, extra=None, comps=(0, 1, 2)):
        f = [field[c, y + 1] for c in comps]
        dy_x = field[comps[0], y + 2] - field[comps[0], y]
        dy_z = field[comps[2], y + 2] - field[comps[2], y]
        dz_x, dz_y = slope_z(f[0]), slope_z(f[1])
        if extra is not None:
            dz_x, dz_y = dz_x + extra[0], dz_y + extra[1]
        return (dy_z - dz_y, dz_x - slope_x(f[2]), slope_x(f[1]) - dy_x), f

    def each_row(body):
        for y in range(n):
            body(y)

    loads[1].wait()
    pltpu.make_async_copy(z_one.at[pl.ds(0, 2)], z_one.at[pl.ds(2, 2)], load_sem.at[3]).wait()
    loads[4].wait()

    def argument(y):
        turn, b = curl(bE, y)
        s = [v[c, y] for c in range(3)]
        sp = gE[SPREAD, y + 1] * (0.5 - 0.5 * (1.0 - iron_factor) * iron[y].astype(jnp.float32))
        gE[1, y + 1] = s[1] * b[2] - s[2] * b[1] - sp * turn[0]
        gE[0, y + 1] = s[2] * b[0] - s[0] * b[2] - sp * turn[1]
        gE[SPREAD, y + 1] = sp
        gE[3, y + 1] = s[0] * b[1] - s[1] * b[0] - sp * turn[2]

    for y in range(cut):
        argument(y)
    start(zg_moves)
    for y in range(cut, n):
        argument(y)
    start(zg_rest)
    start(yg_moves)
    start(yc_moves)

    def local_solve(field, offset):
        def down(k, held):
            m = wide(m_tab[jnp.maximum(k - 1, 0)])
            rows = tuple(field[c, offset + k] + m * held[c] for c in range(3))
            for c in range(3):
                field[c, offset + k] = rows[c]
            return rows

        lax.fori_loop(0, n, down, (zero, zero, zero), unroll=True)

        def up(step, held):
            k = n - 1 - step
            m, inv = wide(m_tab[k]), wide(inv_tab[k])
            rows = tuple(field[c, offset + k] * inv + m * held[c] for c in range(3))
            for c in range(3):
                field[c, offset + k] = rows[c]
            return rows

        lax.fori_loop(0, n, up, (zero, zero, zero), unroll=True)

    left_gap, right_gap = 1.0 - s_low * aa, 1.0 - s_high * aa
    det = 1.0 / (left_gap * right_gap - s_low * s_high * cc * cc)
    ll, lr = right_gap * det, s_low * cc * det
    rr, rl = left_gap * det, s_high * cc * det
    mix[0] = ll * s_low
    mix[1] = lr * s_high
    mix[2] = rl * s_low
    mix[3] = rr * s_high
    low, high = one, one
    for k in range(1, groups):
        chain[0, k] = low
        chain[1, k] = high
        low = low * den_tab[jnp.maximum(me - k, 0)]
        high = high * den_tab[jnp.maximum(groups - 1 - me - k, 0)]
    for k in range(groups - 1):
        below = k < me
        reached = chain[jnp.where(below, 0, 1), jnp.where(below, me - k, k + 1 - me)]
        coef[0, k] = reached * jnp.where(below, ll, lr)
        coef[1, k] = reached * jnp.where(below, rl, rr)

    local_solve(wE, 1)

    def interface(slot, field, offset):
        first = [field[c, offset] for c in range(3)]
        last = [field[c, offset + n - 1] for c in range(3)]
        lefts, rights = [], []
        for c in range(3):
            left = wide(mix[0]) * first[c] + wide(mix[1]) * last[c]
            right = wide(mix[2]) * first[c] + wide(mix[3]) * last[c]
            for k in range(groups - 1):
                end = ends[slot, k, c]
                left = left + wide(coef[0, k]) * end
                right = right + wide(coef[1, k]) * end
            lefts.append(left)
            rights.append(right)
        return lefts, rights

    gather_all(0).wait_recv()
    lefts, rights = interface(0, wE, 1)
    for c in range(3):
        wE[c, 0] = lefts[c]
        wE[c, n + 1] = rights[c]

    def relax(y):
        near, far = wide(al_tab[y]), wide(al_tab[n - 1 - y])
        for c in range(3):
            wE[c, y + 1] = wE[c, y + 1] + near * wE[c, 0] + far * wE[c, n + 1]

    each_row(relax)
    start(zw_moves)

    def pull(y):
        turn, _ = curl(wE, y)
        sp = gE[SPREAD, y + 1]
        for c in range(3):
            tE[c, y] = turn[c]
            hE[c, y + 1] = sp * turn[c]

    each_row(pull)
    start(zh_moves)

    arrive(y_all + z_one_all)
    leave(y_all + z_one_all)

    for side, way in SIDES:
        have = (has_left, has_right)[side]
        edge, halo, y = (1, 0, 0) if side == 0 else (n, n + 1, n - 1)
        beyond, sp = way * y_one[side, NEAR_SPREAD], way * gE[SPREAD, edge]
        g_x = y_one[side, 4] + beyond * (bE[2, edge] + way * rim(yk[side, 0]))
        g_z = y_one[side, 6] - beyond * bE[0, edge]
        gE[1, halo] = jnp.where(have, g_x, 0.0)
        gE[3, halo] = jnp.where(have, g_z, 0.0)
        gE[1, edge] = gE[1, edge] - jnp.where(have, sp * y_one[side, 1], 0.0)
        gE[3, edge] = gE[3, edge] + jnp.where(have, sp * y_one[side, 0], 0.0)
        z_one[3, y] = z_one[3, y] - jnp.where(have, way * z_one[2 + SPREAD, y] * yk[side, 1], 0.0)

    def mend_argument(y):
        sp = gE[SPREAD, y + 1]
        gE[1, y + 1] = gE[1, y + 1] + sp * rim(z_one[1, y])
        gE[0, y + 1] = gE[0, y + 1] - sp * rim(z_one[0, y])

    each_row(mend_argument)

    totals = nothing
    for y in range(n):
        b = [bE[c, y + 1] for c in range(3)]
        sp = z_one[2 + SPREAD, y]
        extra = (
            jnp.where(active, sign * z_one[3, y] - sp * b[1], 0.0),
            jnp.where(active, sign * z_one[2, y] + sp * b[0], 0.0),
        )
        turn, _ = curl(gE, y, extra, G_COMPS)
        rows = [b[c] + half * turn[c] for c in range(3)]
        for c in range(3):
            new[c, y] = rows[c]
        totals = collect(totals, y, rows)
    put_sums(1, totals)
    for copy in gather(1):
        copy.start()

    def pull_field(y):
        turn = [tE[c, y] for c in range(3)]
        s = [v[c, y] for c in range(3)]
        adj[0, y] = wE[0, y + 1] + half * (turn[1] * s[2] - turn[2] * s[1])
        adj[1, y] = wE[1, y + 1] + half * (turn[2] * s[0] - turn[0] * s[2])
        adj[2, y] = wE[2, y + 1] + half * (turn[0] * s[1] - turn[1] * s[0])

    each_row(pull_field)
    wide_inv = wide(r_inv)
    for side, way in SIDES:
        have = (has_left, has_right)[side]
        edge, halo = (1, 0) if side == 0 else (n, n + 1)
        sp = y_one[side, NEAR_SPREAD]
        slope = {}
        for c in (0, 2):
            near, rim_row = wE[c, edge], wE[c, halo]
            outer = rim_row + (rim_row - near) + wide_inv * (rim_row - y_one[side, 2 + c // 2])
            slope[c] = way * (outer - near)
        cross = wE[1, halo]
        hE[0, halo] = jnp.where(have, sp * (slope[2] - slope_z(cross)), 0.0)
        hE[2, halo] = jnp.where(have, sp * (slope_x(cross) - slope[0]), 0.0)

    local_solve(new, 0)
    arrive(z_two_all)
    leave(z_two_all)

    for side, way in SIDES:
        have = (has_left, has_right)[side]
        halo = 0 if side == 0 else n + 1
        hE[0, halo] = hE[0, halo] - jnp.where(have, y_one[side, NEAR_SPREAD] * rim(z_two[1, halo]), 0.0)

    def mend_pull(y):
        c_x, c_y = rim(z_two[0, y + 1]), rim(z_two[1, y + 1])
        sp = gE[SPREAD, y + 1]
        s = [v[c, y] for c in range(3)]
        hE[0, y + 1] = hE[0, y + 1] - sp * c_y
        hE[1, y + 1] = hE[1, y + 1] + sp * c_x
        h_x, h_y = half * c_x, half * c_y
        adj[0, y] = adj[0, y] + h_x * s[2]
        adj[1, y] = adj[1, y] + h_y * s[2]
        adj[2, y] = adj[2, y] - (h_y * s[1] + h_x * s[0])

    each_row(mend_pull)

    def finish_adjoint(y):
        sp = z_one[2 + SPREAD, y]
        extra = (
            jnp.where(active, sign * z_two[0, n + 2 + y] + sp * wE[1, y + 1], 0.0),
            jnp.where(active, sign * z_two[1, n + 2 + y] - sp * wE[0, y + 1], 0.0),
        )
        turn, _ = curl(hE, y, extra)
        for c in range(3):
            adj[c, y] = adj[c, y] - half * turn[c]

    each_row(finish_adjoint)

    gather_all(1).wait_recv()
    lefts, rights = interface(1, new, 0)
    for c in range(3):
        sides[0, c] = lefts[c]
        sides[1, c] = rights[c]

    for slot in range(2):
        gather_all(slot).wait_send()


def hand_over(new, adj, sides, al_tab, new_out, adj_out, done, sem):
    n, nx = done.shape[1], done.shape[3]
    step = 6 if n % 6 == 0 and n <= 24 else n
    adj_copy = pltpu.make_async_copy(adj, adj_out, sem.at[0])
    adj_copy.start()
    copies = []
    for first in range(0, n, step):
        for y in range(first, first + step):
            near, far = (jnp.concatenate([al_tab[k]] * (nx // LANES), axis=1) for k in (y, n - 1 - y))
            for c in range(3):
                done[c, y] = new[c, y] + near * sides[0, c] + far * sides[1, c]
        rows = pl.ds(first, step)
        copies.append(pltpu.make_async_copy(done.at[:, rows], new_out.at[:, rows], sem.at[1 + first // step]))
        copies[-1].start()
    for copy in copies:
        copy.wait()
    adj_copy.wait()


def local(groups, layers, magnetic, velocity, diffusivity, material, plane_rate, cotangent):
    _, n, nz, nx = magnetic.shape
    block = (3, n, nz, nx)
    rimmed = (3, n + 2, nz, nx)
    f32 = jnp.float32
    anywhere = pl.BlockSpec(memory_space=pl.ANY)
    inside = pl.BlockSpec(memory_space=pltpu.VMEM)
    args = [
        pltpu.with_memory_space_constraint(array, pltpu.HBM)
        for array in (magnetic, velocity, diffusivity, material, plane_rate.reshape(1, nz), cotangent)
    ]
    parts = pl.pallas_call(
        functools.partial(kernel, groups, layers, n),
        out_shape=[
            jax.ShapeDtypeStruct(block, f32),
            jax.ShapeDtypeStruct(block, f32),
            jax.ShapeDtypeStruct((2, 3, nz, nx), f32),
            jax.ShapeDtypeStruct((n, nz, LANES), f32),
        ],
        in_specs=[anywhere] * 6,
        out_specs=[inside] * 4,
        scratch_shapes=[
            pltpu.VMEM(rimmed, f32),
            pltpu.VMEM((4, n + 2, nz, nx), f32),
            pltpu.VMEM(rimmed, f32),
            pltpu.VMEM(rimmed, f32),
            pltpu.VMEM(block, f32),
            pltpu.VMEM(block, f32),
            pltpu.VMEM((n, nz, nx), jnp.int32),
            pltpu.VMEM((1, nz), f32),
            pltpu.VMEM((5, n, nz, nx), f32),
            pltpu.VMEM((2, 2 * n + 2, nz, nx), f32),
            pltpu.VMEM((2, 7, nz, nx), f32),
            pltpu.VMEM((2, 2, nz, nx), f32),
            pltpu.VMEM((2, groups - 1, 3, nz, nx), f32),
            pltpu.VMEM((2, 2, 3, nz, nx), f32),
            pltpu.VMEM((n, nz, LANES), f32),
            pltpu.VMEM((n, nz, LANES), f32),
            pltpu.VMEM((groups, nz, LANES), f32),
            pltpu.VMEM((groups, nz, LANES), f32),
            pltpu.VMEM((2, n, nz, LANES), f32),
            pltpu.VMEM((4, nz, LANES), f32),
            pltpu.VMEM((2, groups - 1, nz, LANES), f32),
            pltpu.VMEM((2, groups, nz, LANES), f32),
            pltpu.SemaphoreType.DMA((5,)),
            pltpu.SemaphoreType.DMA((N_WAYS,)),
            pltpu.SemaphoreType.DMA((N_WAYS,)),
            pltpu.SemaphoreType.DMA((2,)),
            pltpu.SemaphoreType.DMA((2,)),
        ],
        compiler_params=pltpu.CompilerParams(
            collective_id=0, has_side_effects=True, vmem_limit_bytes=24 * 2**20
        ),
    )(*args)
    return tuple(pl.pallas_call(
        hand_over,
        out_shape=[jax.ShapeDtypeStruct(block, f32)] * 2,
        in_specs=[inside] * 4,
        out_specs=[anywhere] * 2,
        scratch_shapes=[pltpu.VMEM(block, f32), pltpu.SemaphoreType.DMA((5,))],
        compiler_params=pltpu.CompilerParams(vmem_limit_bytes=2 * 2**20),
    )(*parts))


def solution(mesh):
    in_specs = (
        P(None, "gy", "gz", None),
        P(None, "gy", "gz", None),
        P("gy", "gz", None),
        P("gy", "gz", None),
        P("gz"),
        P(None, "gy", "gz", None),
    )
    out_specs = (P(None, "gy", "gz", None), P(None, "gy", "gz", None))
    body = functools.partial(local, mesh.shape["gy"], mesh.shape["gz"])
    return jax.shard_map(body, mesh=mesh, in_specs=in_specs, out_specs=out_specs, check_vma=False)
```
